256 devices in a mesh: band: 64 (over x, z, core), lev: 4 (over y).
Axes of the slice: x: 4, y: 4, z: 8, core: 2. Of those that a mesh axis runs over, the one named last changes fastest.
Arguments:
- obs_vals: bfloat16 [4, 24, 262144], P('lev', None, 'band'), may hold values from -400 to 400
- obs_colat: bfloat16 [262144], P('band'), may hold values from -1 to 1
- obs_lon: int32 [262144], P('band'), may hold values from 0 to 2047
- band_list: int32 [64, 64, 128], P('band'), may hold values from 0 to 4095, as said below
- counts: int32 [64, 64], P('band'), may hold values from 0 to 128, as said below
- w_in: bfloat16 [96, 256], replicated, may hold values from -0.625 to 0.625
- b_in: float32 [256], replicated, may hold values from -3 to 3
- w_out: bfloat16 [256, 256], P(None, 'lev'), may hold values from -0.375 to 0.375
- b_out: float32 [256], P('lev'), may hold values from -3 to 3
Outputs:
- encoded: bfloat16 [256, 2048, 512], P('lev', 'band')
The draws below stay inside these ranges and needn't reach their ends.
Inputs may be any that keep to these rules, and one draw needn't show every extreme that they name: For each device s and band b the first counts[s, b] entries of band_list[s, b] are indices (within device s) of observations in band b; over all b they name every observation of device s exactly once. Later entries are padding and name arbitrary observations. `counts`: each row sums to 4096. Some band receives 128 observations from every device.
All inputs are finite; a program needn't handle non-finite values.
Results may differ from the reference program's by a relative error of at most 0.0063.
Values may be sent and summed in bfloat16 or wider, within the bound.
A program may use at most 64 MiB of HBM per device.

```python
import math
import jax
import jax.numpy as jnp
from jax import lax

CH_OBS = 24
MLP_HID = 256
OUT_CH = 256
LAT_DEV = 8
LON_DEV = 32
CAP = 128
BANDS = 64
LEVELS = 4
FEAT = 96
NLON = 2048
OBS_DEV = 4096
OBS_TOTAL = 262144


def draw_obs_vals(key, part):
    base_key = jax.random.fold_in(key, 101)
    key_base, key_chan, key_obs = jax.random.split(base_key, 3)
    full_shape = (LEVELS, CH_OBS, OBS_TOTAL)
    base_vals = jnp.clip(jax.random.normal(key_base, full_shape, jnp.float32), -4.0, 4.0)
    log_top = math.log(10.0)
    chan_scale = jnp.exp(jax.random.uniform(key_chan, (LEVELS, CH_OBS, 1), jnp.float32, 0.0, log_top))
    obs_scale = jnp.exp(jax.random.uniform(key_obs, (1, 1, OBS_TOTAL), jnp.float32, 0.0, log_top))
    return (base_vals * chan_scale * obs_scale).astype(jnp.bfloat16)


def routing(key):
    base_key = jax.random.fold_in(key, 202)
    key_order, key_shift, key_perm = jax.random.split(base_key, 3)
    half_cap = CAP // 2
    band_order = jax.random.permutation(key_order, BANDS)
    count_shift = jax.random.randint(key_shift, (BANDS, BANDS // 2), -half_cap, half_cap + 1)
    count_shift = count_shift.at[:, 0].set(half_cap)
    paired = jnp.stack([half_cap + count_shift, half_cap - count_shift], axis=-1).reshape(BANDS, BANDS)
    counts = jnp.zeros((BANDS, BANDS), jnp.int32).at[:, band_order].set(paired.astype(jnp.int32))
    shuffled = jax.vmap(lambda subkey: jax.random.permutation(subkey, OBS_DEV))(jax.random.split(key_perm, BANDS))
    offsets = jnp.cumsum(counts, axis=1) - counts
    slot_index = (offsets[:, :, None] + jnp.arange(CAP, dtype=jnp.int32)[None, None, :]) % OBS_DEV
    band_list = jax.vmap(lambda perm_row, slot_row: perm_row[slot_row])(shuffled, slot_index)
    return (band_list.astype(jnp.int32), counts)


def draw_band_list(key, part):
    return routing(key)[0]


def draw_counts(key, part):
    return routing(key)[1]


def touch_ends(drawn, rng, least, top_value):
    longest = drawn.shape.index(max(drawn.shape))
    spots = []
    for shift in (0, 1):
        where = [jax.random.randint(jax.random.fold_in(rng, axis), (), 0, length) for axis, length in enumerate(drawn.shape)]
        where[longest] = (where[longest] + shift) % drawn.shape[longest]
        spots.append(tuple(where))
    return drawn.at[spots[0]].set(least).at[spots[1]].set(top_value)


def level_of(own_key, shape, pieces, least, top_value):
    factor_of = 1.0
    for position, shards_of in pieces:
        draws = jax.random.uniform(jax.random.fold_in(jax.random.fold_in(own_key, 6), position), (shards_of,), jnp.float32, least / len(pieces), top_value / len(pieces))
        factor_of = factor_of * jnp.repeat(jnp.exp(draws), shape[position] // shards_of).reshape((-1,) + (1,) * (len(shape) - 1 - position))
    return factor_of


def gaussian(rng, shape, spread, reach, cuts=(), kind=jnp.bfloat16):
    loudness = level_of(rng, shape, cuts, -0.22, 0.18) if cuts else 1.0
    entries = jax.random.normal(rng, shape, jnp.float32) * spread * loudness
    return jnp.minimum(jnp.maximum(entries, -reach), reach).astype(kind)


def setup_inputs(seed: int = 0) -> dict:
    streams_of = jax.random.split(jax.random.key(seed), 10)
    return {
        "obs_vals": draw_obs_vals(jax.random.fold_in(streams_of[9], 71), 0),
        "obs_colat": jnp.clip(jax.random.uniform(streams_of[1], (OBS_TOTAL,), jnp.float32, -1.0, 1.0) * level_of(streams_of[1], (OBS_TOTAL,), ((0, 64),), -0.4, 0.0), -1.0, 1.0).astype(jnp.bfloat16),
        "obs_lon": touch_ends(jax.random.randint(streams_of[2], (OBS_TOTAL,), 0, NLON), jax.random.fold_in(streams_of[2], 1), 0, NLON - 1).astype(jnp.int32),
        "band_list": draw_band_list(jax.random.fold_in(streams_of[9], 71), 0),
        "counts": draw_counts(jax.random.fold_in(streams_of[9], 71), 0),
        "w_in": gaussian(streams_of[5], (FEAT, MLP_HID), FEAT ** -0.5, 0.625),
        "b_in": gaussian(streams_of[6], (MLP_HID,), 0.5, 3.0, (), jnp.float32),
        "w_out": gaussian(streams_of[7], (MLP_HID, OUT_CH), MLP_HID ** -0.5, 0.375, ((1, 4),)),
        "b_out": gaussian(streams_of[8], (OUT_CH,), 0.5, 3.0, ((0, 4),), jnp.float32),
    }


norm_eps = 1e-05

def cheb_inverse(nodes):
    order_ids = jnp.arange(nodes, dtype=jnp.float32)[:, None]
    node_ids = jnp.arange(nodes, dtype=jnp.float32)[None, :]
    factor = jnp.where(order_ids == 0.0, 1.0, 2.0).astype(jnp.float32) / nodes
    return (factor * jnp.cos(math.pi * order_ids * (node_ids + 0.5) / nodes)).astype(jnp.float32)

def lat_weights(colat, nodes):
    angles = jnp.arccos(jnp.clip(colat, -1.0, 1.0))
    order_ids = jnp.arange(nodes, dtype=jnp.float32)
    cheb_terms = jnp.cos(order_ids[:, None] * angles[None, :])
    return jnp.dot(cheb_inverse(nodes).T, cheb_terms, precision=lax.Precision.HIGHEST)

def dct_table(length):
    mode_ids = jnp.arange(length, dtype=jnp.float32)[:, None]
    node_ids = jnp.arange(length, dtype=jnp.float32)[None, :]
    row_scale = jnp.where(mode_ids == 0.0, math.sqrt(1.0 / length), math.sqrt(2.0 / length)).astype(jnp.float32)
    return (row_scale * jnp.cos(math.pi * mode_ids * (node_ids + 0.5) / length)).astype(jnp.bfloat16)

def reference(obs_vals, obs_colat, obs_lon, band_list, counts, w_in, b_in, w_out, b_out):
    lat_count = LAT_DEV * BANDS
    lon_count = LON_DEV * BANDS
    slot_ids = jnp.arange(CAP, dtype=jnp.int32)
    live_slot = slot_ids[None, None, :] < counts[:, :, None]
    source_ids = jnp.arange(BANDS, dtype=jnp.int32)[:, None, None] * OBS_DEV + band_list
    target = jnp.where(live_slot, source_ids, OBS_TOTAL).astype(jnp.int32)
    band_ids = jnp.broadcast_to(jnp.arange(BANDS, dtype=jnp.int32)[None, :, None], target.shape)
    obs_band = jnp.zeros((OBS_TOTAL + 1,), jnp.int32).at[target.reshape(-1)].set(band_ids.reshape(-1))[:OBS_TOTAL]
    weights = lat_weights(obs_colat.astype(jnp.float32), LAT_DEV)
    values = obs_vals.reshape(FEAT, OBS_TOTAL)
    node_ids = jnp.arange(LAT_DEV, dtype=jnp.int32)

    def add_source(grid_sum, source):
        first_obs = (source * OBS_DEV).astype(jnp.int32)
        block_vals = lax.dynamic_slice_in_dim(values, first_obs, OBS_DEV, 1).astype(jnp.float32)
        block_weights = lax.dynamic_slice_in_dim(weights, first_obs, OBS_DEV, 1)
        block_band = lax.dynamic_slice_in_dim(obs_band, first_obs, OBS_DEV, 0)
        block_lon = lax.dynamic_slice_in_dim(obs_lon, first_obs, OBS_DEV, 0)
        weighted = (block_vals[:, None, :] * block_weights[None]).astype(jnp.bfloat16)
        weighted = lax.optimization_barrier(weighted).astype(jnp.float32)
        flat_ids = ((block_band[None, :] * LAT_DEV + node_ids[:, None]) * lon_count + block_lon[None, :]).astype(jnp.int32)
        return (grid_sum.at[:, flat_ids].add(weighted), None)
    grid_sum, _ = lax.scan(add_source, jnp.zeros((FEAT, lat_count * lon_count), jnp.float32), jnp.arange(BANDS, dtype=jnp.int32))
    grid_half = grid_sum.reshape(FEAT, lat_count, lon_count).astype(jnp.bfloat16)
    transform = dct_table(lat_count).astype(jnp.float32)
    spectrum = jnp.einsum('fnm,kn->fmk', grid_half.astype(jnp.float32), transform).astype(jnp.bfloat16)
    blocks = spectrum.reshape(FEAT, BANDS, LON_DEV, lat_count).transpose(1, 0, 2, 3)
    w_first = w_in.astype(jnp.float32)
    w_second = w_out.astype(jnp.float32)

    def encode_block(block):
        feats = block.astype(jnp.float32)
        pre_act = jnp.einsum('fh,fmk->hmk', w_first, feats)
        mean_sq = lax.optimization_barrier(jnp.mean(feats * feats, axis=0))
        hidden = jax.nn.gelu(pre_act * lax.rsqrt(mean_sq + norm_eps)[None] + b_in[:, None, None]).astype(jnp.bfloat16)
        output = jnp.einsum('ho,hmk->omk', w_second, hidden.astype(jnp.float32)) + b_out[:, None, None]
        return output.astype(jnp.bfloat16)
    encoded = lax.map(encode_block, blocks)
    return encoded.transpose(1, 0, 2, 3).reshape(OUT_CH, lon_count, lat_count)
```

```python
import functools
import math

import jax
import jax.numpy as jnp
import numpy as np
from jax import lax
from jax.experimental import pallas as pl
from jax.experimental.pallas import tpu as pltpu
from jax.sharding import PartitionSpec as P

LAT = 8
LON = 32
CH = 24
CAP = 128
AUX = 32
LANES = 256
GROUP = 8
STRIDE = 27
EPS = 1e-05
F32, BF16, I32 = jnp.float32, jnp.bfloat16, jnp.int32
MESH = pl.DeviceIdType.MESH


def cheb_inverse():
    order = np.arange(LAT, dtype=np.float64)[:, None]
    node = np.arange(LAT, dtype=np.float64)[None, :]
    factor = np.where(order == 0.0, 1.0, 2.0) / LAT
    return (factor * np.cos(math.pi * order * (node + 0.5) / LAT)).astype(np.float32)


def dct_columns(length):
    mode = np.arange(length, dtype=np.float64)[None, :]
    node = np.arange(length, dtype=np.float64)[:, None]
    scale = np.where(mode == 0.0, math.sqrt(1.0 / length), math.sqrt(2.0 / length))
    return (scale * np.cos(math.pi * mode * (node + 0.5) / length)).astype(np.float32)


def rows_of(value, rows):
    return jnp.broadcast_to(value, (rows, value.shape[1]))


def kernel(
    nb, ny,
    vals, colat, lon, bl, cnt, inv_tab, dct, w_in, b_in, w_out, b_out,
    out,
    table, s1, r1, pm, qm, acc, grid, r2, spec, w1, w2, stage,
    send1, recv1, send2, recv2, send3, recv_l, recv_r, recv_o,
):
    me = lax.axis_index("band")
    lev = lax.axis_index("lev")
    right = lax.rem(lev + 1, ny)
    left = lax.rem(lev + ny - 1, ny)
    opp = lax.rem(lev + 2, ny)
    half_cols = CH * LON // 2
    groups = nb // GROUP
    width = GROUP * CAP
    hid = b_in.shape[0]

    def peer(i):
        return lax.rem(me + i * STRIDE, nb)

    barrier = pltpu.get_barrier_semaphore()

    @pl.loop(1, nb)
    def _(i):
        pl.semaphore_signal(barrier, inc=1, device_id={"band": peer(i)}, device_id_type=MESH)

    for y in (left, right):
        pl.semaphore_signal(barrier, inc=1, device_id={"lev": y}, device_id_type=MESH)

    obs = vals.shape[1]
    pieces = obs // LANES
    lon_v = lon[...]
    row8 = lax.broadcasted_iota(I32, (8, obs), 0)
    aux = jnp.where(
        row8 == 0,
        rows_of(colat[...].astype(F32), 8),
        jnp.where(
            row8 == 1,
            rows_of((lon_v // LON).astype(F32), 8),
            jnp.where(row8 == 2, rows_of((lon_v % LON).astype(F32), 8), 0.0),
        ),
    ).astype(BF16)
    for h in range(pieces):
        table[h * AUX : h * AUX + CH, :] = vals[:, h * LANES : (h + 1) * LANES]
        table[h * AUX + CH : (h + 1) * AUX, :] = aux[:, h * LANES : (h + 1) * LANES]

    batch = 4
    lane = lax.broadcasted_iota(I32, (1, CAP), 1)
    sub = lax.broadcasted_iota(I32, (LANES, CAP), 0)

    def sort_batch(step):
        hots, his = [], []
        for u in range(batch):
            b = peer(step * batch + u)
            idx = bl[pl.ds(b, 1), :]
            live = lane < cnt[pl.ds(b, 1), :]
            his.append(jnp.where(live, idx // LANES, -1))
            hots.append(jnp.where(sub == rows_of(idx % LANES, LANES), 1.0, 0.0).astype(BF16))
        picked = jnp.dot(table[...], jnp.concatenate(hots, 1), preferred_element_type=F32)
        hi = rows_of(jnp.concatenate(his, 1), AUX)
        block = jnp.zeros((AUX, batch * CAP), F32)
        for h in range(pieces):
            block = jnp.where(hi == h, picked[h * AUX : (h + 1) * AUX], block)
        block = block.astype(BF16)
        for u in range(batch):
            s1[step * batch + u] = block[:, u * CAP : (u + 1) * CAP]

    def send_block(i):
        pltpu.make_async_remote_copy(
            src_ref=s1.at[i], dst_ref=r1.at[i],
            send_sem=send1, recv_sem=recv1.at[i // GROUP],
            device_id={"band": peer(i)}, device_id_type=MESH,
        ).start()

    early = nb // batch // 2

    @pl.loop(0, early)
    def _(step):
        sort_batch(step)

    pl.semaphore_wait(barrier, nb - 1 + 2)
    own1 = pltpu.make_async_copy(s1.at[0], r1.at[0], recv1.at[0])
    own1.start()

    @pl.loop(1, early * batch)
    def _(i):
        send_block(i)

    @pl.loop(early, nb // batch)
    def _(step):
        sort_batch(step)
        for u in range(batch):
            send_block(step * batch + u)

    zero = jnp.zeros((CH, hid), F32)
    stacked = []
    for l in range(ny):
        w_l = w_in[l * CH : (l + 1) * CH, :].astype(F32)
        stacked.append(jnp.concatenate([w_l, zero], 1))
        stacked.append(jnp.concatenate([zero, w_l], 1))
    w1[...] = jnp.concatenate(stacked, 0).T.astype(BF16)
    w2[...] = (0.5 * w_out[...].astype(F32)).T.astype(BF16)

    odd8 = (lax.broadcasted_iota(I32, (2 * LAT, CAP), 0) // LAT).astype(F32)
    odd24 = (lax.broadcasted_iota(I32, (2 * CH, CAP), 0) // CH).astype(F32)
    nt = (((1,), (1,)), ((), ()))

    @pl.loop(0, groups)
    def _(g):
        pltpu.make_async_copy(
            s1.at[pl.ds(0, GROUP)], r1.at[pl.ds(0, GROUP)], recv1.at[g]
        ).wait()
        for t in range(GROUP):
            cols = slice(t * CAP, (t + 1) * CAP)
            got = r1[g * GROUP + t]
            tail = got[CH:AUX].astype(F32)
            x, hi, lo = tail[0:1], tail[1:2], tail[2:3]
            weight = rows_of(inv_tab[:, 0:1] * jnp.ones_like(x), LAT) + inv_tab[:, 1:2] * x
            t_prev, t_now = jnp.ones_like(x), x
            for k in range(2, LAT):
                t_prev, t_now = t_now, 2.0 * x * t_now - t_prev
                weight = weight + inv_tab[:, k : k + 1] * t_now
            w_two = jnp.concatenate([weight, weight], 0).astype(BF16)
            v_two = jnp.concatenate([got[0:CH].astype(F32)] * 2, 0).astype(BF16)
            hi_two = (rows_of(hi, 2 * LAT) - odd8).astype(BF16)
            lo_two = (rows_of(lo, 2 * CH) - odd24).astype(BF16)
            none8 = jnp.zeros((2 * LAT, CAP), BF16)
            none24 = jnp.zeros((2 * CH, CAP), BF16)
            for q in range(nb // 2):
                pm[g, q * 2 * LAT : (q + 1) * 2 * LAT, cols] = jnp.where(
                    hi_two == jnp.asarray(2.0 * q, BF16), w_two, none8
                )
            for q in range(LON // 2):
                qm[g, q * 2 * CH : (q + 1) * 2 * CH, cols] = jnp.where(
                    lo_two == jnp.asarray(2.0 * q, BF16), v_two, none24
                )
        part = lax.dot_general(pm[g], qm[g, 0:half_cols], nt, preferred_element_type=F32)

        @pl.when(g == 0)
        def _():
            acc[...] = part

        @pl.when(g > 0)
        def _():
            acc[...] += part

    def send_grid(h):
        grid[h] = acc[...].reshape(nb, LAT, half_cols).astype(BF16)
        pltpu.make_async_copy(grid.at[h, me], r2.at[h, me], recv2.at[h]).start()

        @pl.loop(1, nb)
        def _(i):
            to = peer(i)
            pltpu.make_async_remote_copy(
                src_ref=grid.at[h, to], dst_ref=r2.at[h, me],
                send_sem=send2.at[h], recv_sem=recv2.at[h],
                device_id={"band": to}, device_id_type=MESH,
            ).start()

    send_grid(0)

    @pl.loop(0, groups)
    def _(g):
        part = lax.dot_general(
            pm[g], qm[g, half_cols : 2 * half_cols], nt, preferred_element_type=F32
        )

        @pl.when(g == 0)
        def _():
            acc[...] = part

        @pl.when(g > 0)
        def _():
            acc[...] += part

    send_grid(1)

    def transform(h):
        pltpu.make_async_copy(grid.at[h], r2.at[h], recv2.at[h]).wait()
        nodes = r2[h].astype(F32).reshape(nb * LAT, half_cols).astype(BF16)
        modes = lax.dot_general(
            nodes, dct[...], (((0,), (0,)), ((), ())), preferred_element_type=F32
        )
        spec[lev, h * half_cols : (h + 1) * half_cols, :] = modes.astype(BF16)

    chunks = 8
    rows = CH * LON // chunks

    def piece(level, i):
        return spec.at[level, i * rows : (i + 1) * rows]

    def push(level, i, to, sem):
        pltpu.make_async_remote_copy(
            src_ref=piece(level, i), dst_ref=piece(level, i),
            send_sem=send3, recv_sem=sem.at[i],
            device_id={"lev": to}, device_id_type=MESH,
        ).start()

    def arrived(level, i, sem):
        pltpu.make_async_copy(piece(level, i), piece(level, i), sem.at[i]).wait()

    def own(i):
        push(lev, i, right, recv_l)
        push(lev, i, left, recv_r)

    def relay(i):
        arrived(left, i, recv_l)
        if i % 2 == 0:
            push(left, i, right, recv_o)
        arrived(right, i, recv_r)
        if i % 2 == 1:
            push(right, i, left, recv_o)

    def encode(i):
        arrived(opp, i, recv_o)
        pairs = rows // (2 * CH)
        for p in range(i * pairs, (i + 1) * pairs):
            feats = spec[:, p * 2 * CH : (p + 1) * 2 * CH, :]
            wide = feats.astype(F32)
            square = jnp.sum(wide * wide, axis=0)
            pre = jnp.dot(
                w1[...], feats.reshape(ny * 2 * CH, feats.shape[2]), preferred_element_type=F32
            )
            for par in range(2):
                mean = jnp.sum(square[par * CH : (par + 1) * CH], axis=0, keepdims=True)
                norm = lax.rsqrt(mean * (1.0 / (ny * CH)) + EPS)
                z = pre[par * hid : (par + 1) * hid] * norm + b_in[...]
                bend = jnp.tanh(z * (0.7978845608028654 + 0.035677408136300125 * (z * z)))
                hidden = (z + z * bend).astype(BF16)
                stage[:, 2 * p + par, :] = (
                    jnp.dot(w2[...], hidden, preferred_element_type=F32) + b_out[...]
                )
        done = LON // chunks
        if i % 2 == 1:
            lo_m, hi_m = (i - 1) * done, (i + 1) * done
            out[:, lo_m:hi_m, :] = stage[:, lo_m:hi_m, :].astype(BF16)

    half = chunks // 2
    transform(0)
    for i in range(half):
        own(i)
    for i in range(half):
        relay(i)
    transform(1)
    for i in range(half, chunks):
        own(i)
    for i in range(half):
        encode(i)
        relay(half + i)
    for i in range(half, chunks):
        encode(i)

    pltpu.make_async_copy(s1.at[pl.ds(0, nb - 1)], r1.at[pl.ds(0, nb - 1)], send1).wait()
    for h in range(2):
        sent = grid.at[h, pl.ds(0, nb - 1)]
        pltpu.make_async_copy(sent, sent, send2.at[h]).wait()
    sent = spec.at[pl.ds(0, 3)]
    pltpu.make_async_copy(sent, sent, send3).wait()


def on_device(nb, ny, obs_vals, obs_colat, obs_lon, band_list, counts, w_in, b_in, w_out, b_out):
    obs = obs_vals.shape[2]
    modes = nb * LAT
    outs = w_out.shape[1]
    half_cols = CH * LON // 2
    groups = nb // GROUP
    width = GROUP * CAP
    dma = pltpu.SemaphoreType.DMA
    vmem = pl.BlockSpec(memory_space=pltpu.VMEM)
    return pl.pallas_call(
        functools.partial(kernel, nb, ny),
        out_shape=jax.ShapeDtypeStruct((outs, LON, modes), BF16),
        in_specs=[vmem] * 11,
        out_specs=vmem,
        scratch_shapes=[
            pltpu.VMEM((obs // LANES * AUX, LANES), BF16),
            pltpu.VMEM((nb, AUX, CAP), BF16),
            pltpu.VMEM((nb, AUX, CAP), BF16),
            pltpu.VMEM((groups, nb * LAT, width), BF16),
            pltpu.VMEM((groups, LON * CH, width), BF16),
            pltpu.VMEM((nb * LAT, half_cols), F32),
            pltpu.VMEM((2, nb, LAT, half_cols), BF16),
            pltpu.VMEM((2, nb, LAT, half_cols), BF16),
            pltpu.VMEM((ny, LON * CH, modes), BF16),
            pltpu.VMEM((2 * w_in.shape[1], 2 * w_in.shape[0]), BF16),
            pltpu.VMEM((outs, w_out.shape[0]), BF16),
            pltpu.VMEM((outs, LON, modes), F32),
            dma, dma((groups,)), dma((2,)), dma((2,)), dma, dma((8,)), dma((8,)), dma((8,)),
        ],
        compiler_params=pltpu.CompilerParams(
            collective_id=0, has_side_effects=True, vmem_limit_bytes=62 * 1024 * 1024
        ),
    )(
        obs_vals[0],
        obs_colat[None, :],
        obs_lon[None, :],
        band_list[0],
        counts.reshape(nb, 1),
        jnp.asarray(cheb_inverse().T),
        jnp.asarray(dct_columns(modes)).astype(BF16),
        w_in,
        b_in[:, None],
        w_out,
        b_out[:, None],
    )


def solution(mesh):
    nb, ny = mesh.shape["band"], mesh.shape["lev"]
    in_specs = (
        P("lev", None, "band"),
        P("band"),
        P("band"),
        P("band", None, None),
        P("band", None),
        P(),
        P(),
        P(None, "lev"),
        P("lev"),
    )
    return jax.shard_map(
        functools.partial(on_device, nb, ny),
        mesh=mesh, in_specs=in_specs, out_specs=P("lev", "band", None), check_vma=False,
    )
```

```python
import functools
import math

import jax
import jax.numpy as jnp
import numpy as np
from jax import lax
from jax.experimental import pallas as pl
from jax.experimental.pallas import tpu as pltpu
from jax.sharding import PartitionSpec as P

LAT = 8
LON = 32
CH = 24
CAP = 128
AUX = 32
LANES = 256
INPUTS = 11
GROUP = 8
STRIDE = 27
PARTS = 3
SPLIT = 2
DEPTH = 8
PIECES = 12
ROWS = 16
EPS = 1e-05
F32, BF16, I32 = jnp.float32, jnp.bfloat16, jnp.int32
MESH = pl.DeviceIdType.MESH


def cheb_inverse():
    order = np.arange(LAT, dtype=np.float64)[:, None]
    node = np.arange(LAT, dtype=np.float64)[None, :]
    factor = np.where(order == 0.0, 1.0, 2.0) / LAT
    return (factor * np.cos(math.pi * order * (node + 0.5) / LAT)).astype(np.float32)


def dct_columns(length):
    mode = np.arange(length, dtype=np.float64)[None, :]
    node = np.arange(length, dtype=np.float64)[:, None]
    scale = np.where(mode == 0.0, math.sqrt(1.0 / length), math.sqrt(2.0 / length))
    return (scale * np.cos(math.pi * mode * (node + 0.5) / length)).astype(np.float32)


def rows_of(value, rows):
    return jnp.broadcast_to(value, (rows, value.shape[1]))


def kernel(
    nb, ny,
    *refs,
):
    hbm, out, local = refs[:INPUTS], refs[INPUTS], refs[INPUTS + 1 : 2 * INPUTS + 1]
    vals, colat, lon, bl, cnt, inv_tab, dct, w_in, b_in, w_out, b_out = local
    (
        live_n, bias1, bias2, table, s1, r1, prep, acc, grid, r2, spec, w1, w2, pre, stage,
        load, send1, recv1, send2, recv2, send3, recv_l, recv_r, recv_o,
    ) = refs[2 * INPUTS + 1 :]
    me = lax.axis_index("band")
    lev = lax.axis_index("lev")
    right = lax.rem(lev + 1, ny)
    left = lax.rem(lev + ny - 1, ny)
    opp = lax.rem(lev + 2, ny)
    part_cols = CH * LON // PARTS
    send_cols = part_cols // SPLIT
    groups = nb // GROUP
    hid = b_in.shape[1]

    def peer(i):
        return lax.rem(me + i * STRIDE, nb)

    loads = [pltpu.make_async_copy(hbm[k], local[k], load.at[k]) for k in range(INPUTS)]
    for copy in loads:
        copy.start()
    barrier = pltpu.get_barrier_semaphore()

    @pl.loop(1, nb)
    def _(i):
        pl.semaphore_signal(barrier, inc=1, device_id={"band": peer(i)}, device_id_type=MESH)

    for y in (left, right):
        pl.semaphore_signal(barrier, inc=1, device_id={"lev": y}, device_id_type=MESH)

    for copy in loads:
        copy.wait()
    for row, column in ((cnt, live_n), (b_in, bias1), (b_out, bias2)):
        n, copies = row.shape[1], column.shape[1]
        r_id = lax.broadcasted_iota(I32, (n, n), 0)
        c_id = lax.broadcasted_iota(I32, (n, n), 1)
        wide_row = rows_of(row[...].astype(F32), n)
        one = jnp.sum(jnp.where(r_id == c_id, wide_row, 0.0), axis=1, keepdims=True)
        column[...] = jnp.broadcast_to(one, (n, copies))

    obs = vals.shape[1]
    pieces = obs // LANES
    lon_v = lon[...]
    lon_hi, lon_lo = (lon_v // LON).astype(F32), (lon_v % LON).astype(F32)
    pos = colat[...].astype(F32)
    row8 = lax.broadcasted_iota(I32, (8, CAP), 0)
    for h in range(pieces):
        table[h * AUX : h * AUX + CH, :] = vals[:, h * LANES : (h + 1) * LANES]
        for part in range(LANES // CAP):
            r = h * (LANES // CAP) + part
            aux = jnp.zeros((8, CAP), F32)
            for k, source in enumerate((pos, lon_hi, lon_lo)):
                aux = jnp.where(row8 == k, rows_of(source[r : r + 1], 8), aux)
            table[h * AUX + CH : (h + 1) * AUX, part * CAP : (part + 1) * CAP] = aux.astype(BF16)

    batch = 4
    lane = lax.broadcasted_iota(I32, (1, CAP), 1)
    sub = lax.broadcasted_iota(I32, (LANES, CAP), 0)

    def sort_batch(step):
        hots, his = [], []
        for u in range(batch):
            b = peer(step * batch + u)
            idx = bl[pl.ds(b, 1), :]
            live = lane.astype(F32) < live_n[pl.ds(b, 1), :]
            his.append(jnp.where(live, idx // LANES, -1))
            hots.append(jnp.where(sub == rows_of(idx % LANES, LANES), 1.0, 0.0).astype(BF16))
        picked = jnp.dot(table[...], jnp.concatenate(hots, 1), preferred_element_type=F32)
        hi = rows_of(jnp.concatenate(his, 1), AUX)
        block = jnp.zeros((AUX, batch * CAP), F32)
        for h in range(pieces):
            block = jnp.where(hi == h, picked[h * AUX : (h + 1) * AUX], block)
        block = block.astype(BF16)
        for u in range(batch):
            s1[step * batch + u] = block[:, u * CAP : (u + 1) * CAP]

    def send_block(i):
        pltpu.make_async_remote_copy(
            src_ref=s1.at[i], dst_ref=r1.at[i],
            send_sem=send1, recv_sem=recv1.at[i // GROUP],
            device_id={"band": peer(i)}, device_id_type=MESH,
        ).start()

    @pl.loop(0, nb // batch)
    def _(step):
        sort_batch(step)

    pl.semaphore_wait(barrier, nb - 1 + 2)
    pltpu.make_async_copy(s1.at[0], r1.at[0], recv1.at[0]).start()

    @pl.loop(1, nb)
    def _(i):
        send_block(i)

    zero = jnp.zeros((CH, hid), F32)
    stacked = []
    for l in range(ny):
        w_l = w_in[l * CH : (l + 1) * CH, :].astype(F32)
        stacked.append(jnp.concatenate([w_l, zero], 1))
        stacked.append(jnp.concatenate([zero, w_l], 1))
    w1[...] = jnp.concatenate(stacked, 0).T.astype(BF16)
    w2[...] = (0.5 * w_out[...].astype(F32)).astype(BF16)

    odd8 = (lax.broadcasted_iota(I32, (2 * LAT, CAP), 0) // LAT).astype(F32)
    odd24 = (lax.broadcasted_iota(I32, (2 * CH, CAP), 0) // CH).astype(F32)
    nt = (((1,), (1,)), ((), ()))

    def add_part(n, g):
        total = None
        for first in range(0, GROUP, DEPTH):
            lefts, rights = [], []
            for t in range(first, first + DEPTH):
                block = prep[g * GROUP + t].astype(BF16)
                hi_two, w_two = block[0 : 2 * LAT], block[2 * LAT : 4 * LAT]
                none = jnp.zeros_like(w_two)
                lefts.append(
                    jnp.concatenate(
                        [
                            jnp.where(hi_two == jnp.asarray(2.0 * q, BF16), w_two, none)
                            for q in range(nb // 2)
                        ]
                    )
                )
                tiles = []
                for tile in range(n * part_cols // 16, (n + 1) * part_cols // 16):
                    q, third = divmod(tile, 3)
                    at = 4 * LAT + 16 * third
                    tiles.append(
                        jnp.where(
                            block[at : at + 16] == jnp.asarray(2.0 * q, BF16),
                            block[at + 2 * CH : at + 2 * CH + 16],
                            none,
                        )
                    )
                rights.append(jnp.concatenate(tiles))
            term = lax.dot_general(
                jnp.concatenate(lefts, 1), jnp.concatenate(rights, 1), nt,
                preferred_element_type=F32,
            )
            total = term if total is None else total + term
        acc[...] += total

    clear = jnp.zeros(acc.shape, F32)
    columns = [jnp.broadcast_to(inv_tab[:, k : k + 1], (LAT, CAP)) for k in range(LAT)]
    acc[...] = clear

    @pl.loop(0, groups)
    def _(g):
        pltpu.make_async_copy(
            s1.at[pl.ds(0, GROUP)], r1.at[pl.ds(0, GROUP)], recv1.at[g]
        ).wait()
        for t in range(GROUP):
            got = r1[g * GROUP + t]
            tail = got[CH:AUX].astype(F32)
            x, hi, lo = tail[0:1], tail[1:2], tail[2:3]
            weight = columns[0] + columns[1] * x
            t_prev, t_now = jnp.ones_like(x), x
            for k in range(2, LAT):
                t_prev, t_now = t_now, 2.0 * x * t_now - t_prev
                weight = weight + columns[k] * t_now
            values = got[0:CH].astype(F32)
            prep[g * GROUP + t] = jnp.concatenate(
                [rows_of(hi, 2 * LAT) - odd8, weight, weight, rows_of(lo, 2 * CH) - odd24, values, values]
            )
        add_part(0, g)

    def send_grid(n):
        for s in range(n * SPLIT, (n + 1) * SPLIT):
            cols = slice((s - n * SPLIT) * send_cols, (s - n * SPLIT + 1) * send_cols)
            grid[s] = acc[:, cols].reshape(nb, LAT, send_cols).astype(BF16)
            pltpu.make_async_copy(grid.at[s, me], r2.at[s, me], recv2.at[s]).start()

            @pl.loop(1, nb)
            def _(i):
                to = peer(i)
                pltpu.make_async_remote_copy(
                    src_ref=grid.at[s, to], dst_ref=r2.at[s, me],
                    send_sem=send2.at[s], recv_sem=recv2.at[s],
                    device_id={"band": to}, device_id_type=MESH,
                ).start()

    send_grid(0)
    for n in range(1, PARTS):
        acc[...] = clear

        @pl.loop(0, groups)
        def _(g):
            add_part(n, g)

        send_grid(n)

    def transform(n):
        pltpu.make_async_copy(grid.at[n], r2.at[n], recv2.at[n]).wait()
        nodes = r2[n].astype(F32).reshape(nb * LAT, send_cols).astype(BF16)
        modes = lax.dot_general(
            nodes, dct[...], (((0,), (0,)), ((), ())), preferred_element_type=F32
        )
        spec[lev, n * send_cols : (n + 1) * send_cols, :] = modes.astype(BF16)

    rows = CH * LON // PIECES

    def piece(level, i):
        return spec.at[level, i * rows : (i + 1) * rows]

    def push(level, i, to, sem):
        pltpu.make_async_remote_copy(
            src_ref=piece(level, i), dst_ref=piece(level, i),
            send_sem=send3, recv_sem=sem.at[i],
            device_id={"lev": to}, device_id_type=MESH,
        ).start()

    def arrived(level, i, sem):
        pltpu.make_async_copy(piece(level, i), piece(level, i), sem.at[i]).wait()

    def own(i):
        push(lev, i, right, recv_l)
        push(lev, i, left, recv_r)

    def relay(i):
        if i % 2 == 0:
            arrived(left, i, recv_l)
            push(left, i, right, recv_o)
        else:
            arrived(right, i, recv_r)
            push(right, i, left, recv_o)

    def encode(p):
        first = pl.multiple_of(p * 2 * CH, 2 * CH)
        feats = spec[:, pl.ds(first, 2 * CH), :]
        modes = feats.shape[2]
        wide = feats.astype(F32)
        square = jnp.sum(wide * wide, axis=0)
        pre[...] = jnp.dot(
            w1[...], feats.reshape(ny * 2 * CH, modes), preferred_element_type=F32
        )
        for par in range(2):
            mean = jnp.sum(square[par * CH : (par + 1) * CH], axis=0, keepdims=True)
            norm = rows_of(lax.rsqrt(mean * (1.0 / (ny * CH)) + EPS), ROWS)
            act = []
            for r in range(0, hid, ROWS):
                bias = jnp.concatenate([bias1[r : r + ROWS, :]] * (modes // CAP), 1)
                z = pre[par * hid + r : par * hid + r + ROWS, :] * norm + bias
                bend = jnp.tanh(z * (0.7978845608028654 + 0.035677408136300125 * (z * z)))
                act.append((z + z * bend).astype(BF16))
            stage[:, 2 * p + par, :] = (
                jnp.dot(w2[...], jnp.concatenate(act), preferred_element_type=F32) + bias2[...]
            )

    ready = [(i + 1) * rows // (2 * CH) for i in range(PIECES)]

    def encode_piece(i):
        if i % 2 == 0:
            arrived(right, i, recv_r)
        else:
            arrived(left, i, recv_l)
        arrived(opp, i, recv_o)
        before = ready[i - 1] if i else 0

        @pl.loop(before, ready[i])
        def _(p):
            encode(p)

        lo_m, hi_m = before * 2 // 8 * 8, ready[i] * 2 // 8 * 8
        if hi_m > lo_m:
            out[:, lo_m:hi_m, :] = stage[:, lo_m:hi_m, :].astype(BF16)

    for n in range(PARTS * SPLIT):
        transform(n)
        own(2 * n)
        own(2 * n + 1)
        if n in (1, 2, 3):
            relay(2 * n - 2)
            relay(2 * n - 1)
    encode_piece(0)
    encode_piece(1)
    relay(6)
    relay(7)
    encode_piece(2)
    encode_piece(3)
    relay(8)
    relay(9)
    for i in range(4, 8):
        encode_piece(i)
    relay(10)
    relay(11)
    for i in range(8, PIECES):
        encode_piece(i)

    pltpu.make_async_copy(s1.at[pl.ds(0, nb - 1)], r1.at[pl.ds(0, nb - 1)], send1).wait()
    for h in range(PARTS * SPLIT):
        sent = grid.at[h, pl.ds(0, nb - 1)]
        pltpu.make_async_copy(sent, sent, send2.at[h]).wait()
    sent = spec.at[pl.ds(0, 3)]
    pltpu.make_async_copy(sent, sent, send3).wait()


def on_device(nb, ny, obs_vals, obs_colat, obs_lon, band_list, counts, w_in, b_in, w_out, b_out):
    obs = obs_vals.shape[2]
    modes = nb * LAT
    outs = w_out.shape[1]
    part_cols = CH * LON // PARTS
    send_cols = part_cols // SPLIT
    groups = nb // GROUP
    dma = pltpu.SemaphoreType.DMA
    vmem = pl.BlockSpec(memory_space=pltpu.VMEM)
    args = (
        obs_vals[0],
        obs_colat.reshape(obs // CAP, CAP),
        obs_lon.reshape(obs // CAP, CAP),
        band_list[0],
        counts,
        jnp.asarray(cheb_inverse().T),
        jnp.asarray(dct_columns(modes)).astype(BF16),
        w_in,
        b_in[None, :],
        w_out.T,
        b_out[None, :],
    )
    return pl.pallas_call(
        functools.partial(kernel, nb, ny),
        out_shape=jax.ShapeDtypeStruct((outs, LON, modes), BF16),
        in_specs=[pl.BlockSpec(memory_space=pltpu.HBM)] * INPUTS,
        out_specs=vmem,
        scratch_shapes=[
            *(pltpu.VMEM(arg.shape, arg.dtype) for arg in args),
            pltpu.VMEM((nb, 1), F32),
            pltpu.VMEM((w_in.shape[1], CAP), F32),
            pltpu.VMEM((outs, 1), F32),
            pltpu.VMEM((obs // LANES * AUX, LANES), BF16),
            pltpu.VMEM((nb, AUX, CAP), BF16),
            pltpu.VMEM((nb, AUX, CAP), BF16),
            pltpu.VMEM((nb, 4 * LAT + 4 * CH, CAP), F32),
            pltpu.VMEM((nb * LAT, part_cols), F32),
            pltpu.VMEM((PARTS * SPLIT, nb, LAT, send_cols), BF16),
            pltpu.VMEM((PARTS * SPLIT, nb, LAT, send_cols), BF16),
            pltpu.VMEM((ny, LON * CH, modes), BF16),
            pltpu.VMEM((2 * w_in.shape[1], 2 * w_in.shape[0]), BF16),
            pltpu.VMEM((outs, w_out.shape[0]), BF16),
            pltpu.VMEM((2 * w_in.shape[1], modes), F32),
            pltpu.VMEM((outs, LON, modes), F32),
            dma((INPUTS,)), dma, dma((groups,)), dma((PARTS * SPLIT,)), dma((PARTS * SPLIT,)),
            dma, dma((PIECES,)), dma((PIECES,)), dma((PIECES,)),
        ],
        compiler_params=pltpu.CompilerParams(
            collective_id=0, has_side_effects=True, vmem_limit_bytes=40 * 1024 * 1024
        ),
    )(*(pltpu.with_memory_space_constraint(arg, pltpu.HBM) for arg in args))


def solution(mesh):
    nb, ny = mesh.shape["band"], mesh.shape["lev"]
    in_specs = (
        P("lev", None, "band"),
        P("band"),
        P("band"),
        P("band", None, None),
        P("band", None),
        P(),
        P(),
        P(None, "lev"),
        P("lev"),
    )
    return jax.shard_map(
        functools.partial(on_device, nb, ny),
        mesh=mesh, in_specs=in_specs, out_specs=P("lev", "band", None), check_vma=False,
    )
```

```python
import functools
import math

import jax
import jax.numpy as jnp
import numpy as np
from jax import lax
from jax.experimental import pallas as pl
from jax.experimental.pallas import tpu as pltpu
from jax.sharding import PartitionSpec as P

LAT = 8
LON = 32
CH = 24
CAP = 128
AUX = 32
LANES = 256
INPUTS = 11
GROUP = 8
STRIDE = 27
PARTS = 3
SPLIT = 2
DEPTH = 8
PIECES = 12
STRIPS = 1
ROWS = 16
EPS = 1e-05
F32, BF16, I32 = jnp.float32, jnp.bfloat16, jnp.int32
MESH = pl.DeviceIdType.MESH


def cheb_inverse():
    order = np.arange(LAT, dtype=np.float64)[:, None]
    node = np.arange(LAT, dtype=np.float64)[None, :]
    factor = np.where(order == 0.0, 1.0, 2.0) / LAT
    return (factor * np.cos(math.pi * order * (node + 0.5) / LAT)).astype(np.float32)


def dct_columns(length):
    mode = np.arange(length, dtype=np.float64)[None, :]
    node = np.arange(length, dtype=np.float64)[:, None]
    scale = np.where(mode == 0.0, math.sqrt(1.0 / length), math.sqrt(2.0 / length))
    return (scale * np.cos(math.pi * mode * (node + 0.5) / length)).astype(np.float32)


def rows_of(value, rows):
    return jnp.broadcast_to(value, (rows, value.shape[1]))


def kernel(
    nb, ny,
    *refs,
):
    hbm, out, local = refs[:INPUTS], refs[INPUTS], refs[INPUTS + 1 : 2 * INPUTS + 1]
    vals, colat, lon, bl, cnt, inv_tab, dct, w_in, b_in, w_out, b_out = local
    (
        live_n, bias2, table, s1, r1, prep, acc, grid, r2, spec, w1, w2, pre, stage,
        load, send1, recv1, send2, recv2, send3, recv_l, recv_r, recv_o,
    ) = refs[2 * INPUTS + 1 :]
    me = lax.axis_index("band")
    lev = lax.axis_index("lev")
    right = lax.rem(lev + 1, ny)
    left = lax.rem(lev + ny - 1, ny)
    opp = lax.rem(lev + 2, ny)
    part_cols = CH * LON // PARTS
    send_cols = part_cols // SPLIT
    groups = nb // GROUP
    hid = b_in.shape[1]

    def peer(i):
        return lax.rem(me + i * STRIDE, nb)

    loads = [pltpu.make_async_copy(hbm[k], local[k], load.at[k]) for k in range(INPUTS)]
    for copy in loads:
        copy.start()
    barrier = pltpu.get_barrier_semaphore()

    @pl.loop(1, nb)
    def _(i):
        pl.semaphore_signal(barrier, inc=1, device_id={"band": peer(i)}, device_id_type=MESH)

    for y in (left, right):
        pl.semaphore_signal(barrier, inc=1, device_id={"lev": y}, device_id_type=MESH)

    for copy in loads:
        copy.wait()
    for row, column in ((cnt, live_n), (b_out, bias2)):
        n, copies = row.shape[1], column.shape[1]
        r_id = lax.broadcasted_iota(I32, (n, n), 0)
        c_id = lax.broadcasted_iota(I32, (n, n), 1)
        wide_row = rows_of(row[...].astype(F32), n)
        one = jnp.sum(jnp.where(r_id == c_id, wide_row, 0.0), axis=1, keepdims=True)
        column[...] = jnp.broadcast_to(one, (n, copies))

    obs = vals.shape[1]
    pieces = obs // LANES
    lon_v = lon[...]
    lon_hi, lon_lo = (lon_v // LON).astype(F32), (lon_v % LON).astype(F32)
    pos = colat[...].astype(F32)
    row8 = lax.broadcasted_iota(I32, (8, CAP), 0)
    for h in range(pieces):
        table[h * AUX : h * AUX + CH, :] = vals[:, h * LANES : (h + 1) * LANES]
        for part in range(LANES // CAP):
            r = h * (LANES // CAP) + part
            aux = jnp.zeros((8, CAP), F32)
            for k, source in enumerate((pos, lon_hi, lon_lo)):
                aux = jnp.where(row8 == k, rows_of(source[r : r + 1], 8), aux)
            table[h * AUX + CH : (h + 1) * AUX, part * CAP : (part + 1) * CAP] = aux.astype(BF16)

    batch = 4
    lane = lax.broadcasted_iota(I32, (1, CAP), 1)
    sub = lax.broadcasted_iota(I32, (LANES, CAP), 0)

    def sort_batch(step):
        hots, his = [], []
        for u in range(batch):
            b = peer(step * batch + u)
            idx = bl[pl.ds(b, 1), :]
            live = lane.astype(F32) < live_n[pl.ds(b, 1), :]
            his.append(jnp.where(live, idx // LANES, -1))
            hots.append(jnp.where(sub == rows_of(idx % LANES, LANES), 1.0, 0.0).astype(BF16))
        picked = jnp.dot(table[...], jnp.concatenate(hots, 1), preferred_element_type=F32)
        hi = rows_of(jnp.concatenate(his, 1), AUX)
        block = jnp.zeros((AUX, batch * CAP), F32)
        for h in range(pieces):
            block = jnp.where(hi == h, picked[h * AUX : (h + 1) * AUX], block)
        block = block.astype(BF16)
        for u in range(batch):
            s1[step * batch + u] = block[:, u * CAP : (u + 1) * CAP]

    def send_block(i):
        pltpu.make_async_remote_copy(
            src_ref=s1.at[i], dst_ref=r1.at[i],
            send_sem=send1, recv_sem=recv1.at[i // GROUP],
            device_id={"band": peer(i)}, device_id_type=MESH,
        ).start()

    early = nb // batch * 3 // 4

    @pl.loop(0, early)
    def _(step):
        sort_batch(step)

    pl.semaphore_wait(barrier, nb - 1 + 2)
    pltpu.make_async_copy(s1.at[0], r1.at[0], recv1.at[0]).start()

    @pl.loop(1, early * batch)
    def _(i):
        send_block(i)

    @pl.loop(early, nb // batch)
    def _(step):
        sort_batch(step)
        for u in range(batch):
            send_block(step * batch + u)

    zero = jnp.zeros((CH, hid), F32)
    stacked = []
    for l in range(ny):
        w_l = w_in[l * CH : (l + 1) * CH, :].astype(F32)
        stacked.append(jnp.concatenate([w_l, zero], 1))
        stacked.append(jnp.concatenate([zero, w_l], 1))
    bias = jnp.concatenate([b_in[...]] * 2, 1)
    coarse = bias.astype(BF16).astype(F32)
    row16 = lax.broadcasted_iota(I32, (16, 2 * hid), 0)
    stacked.append(
        jnp.where(row16 == 0, rows_of(coarse, 16), jnp.where(row16 == 1, rows_of(bias - coarse, 16), 0.0))
    )
    w1[...] = jnp.concatenate(stacked, 0).T.astype(BF16)
    w2[...] = (0.5 * w_out[...].astype(F32)).astype(BF16)

    odd8 = (lax.broadcasted_iota(I32, (2 * LAT, CAP), 0) // LAT).astype(F32)
    odd24 = (lax.broadcasted_iota(I32, (2 * CH, CAP), 0) // CH).astype(F32)
    nt = (((1,), (1,)), ((), ()))

    def add_part(n, g):
        total = None
        for first in range(0, GROUP, DEPTH):
            lefts, rights = [], []
            for t in range(first, first + DEPTH):
                block = prep[g * GROUP + t].astype(BF16)
                hi_two, w_two = block[0 : 2 * LAT], block[2 * LAT : 4 * LAT]
                none = jnp.zeros_like(w_two)
                lefts.append(
                    jnp.concatenate(
                        [
                            jnp.where(hi_two == jnp.asarray(2.0 * q, BF16), w_two, none)
                            for q in range(nb // 2)
                        ]
                    )
                )
                tiles = []
                for tile in range(n * part_cols // 16, (n + 1) * part_cols // 16):
                    q, third = divmod(tile, 3)
                    at = 4 * LAT + 16 * third
                    tiles.append(
                        jnp.where(
                            block[at : at + 16] == jnp.asarray(2.0 * q, BF16),
                            block[at + 2 * CH : at + 2 * CH + 16],
                            none,
                        )
                    )
                rights.append(jnp.concatenate(tiles))
            term = lax.dot_general(
                jnp.concatenate(lefts, 1), jnp.concatenate(rights, 1), nt,
                preferred_element_type=F32,
            )
            total = term if total is None else total + term
        acc[...] += total

    clear = jnp.zeros(acc.shape, F32)
    columns = [jnp.broadcast_to(inv_tab[:, k : k + 1], (LAT, CAP)) for k in range(LAT)]
    acc[...] = clear

    @pl.loop(0, groups)
    def _(g):
        pltpu.make_async_copy(
            s1.at[pl.ds(0, GROUP)], r1.at[pl.ds(0, GROUP)], recv1.at[g]
        ).wait()
        for t in range(GROUP):
            got = r1[g * GROUP + t]
            tail = got[CH:AUX].astype(F32)
            x, hi, lo = tail[0:1], tail[1:2], tail[2:3]
            weight = columns[0] + columns[1] * x
            t_prev, t_now = jnp.ones_like(x), x
            for k in range(2, LAT):
                t_prev, t_now = t_now, 2.0 * x * t_now - t_prev
                weight = weight + columns[k] * t_now
            values = got[0:CH].astype(F32)
            prep[g * GROUP + t] = jnp.concatenate(
                [rows_of(hi, 2 * LAT) - odd8, weight, weight, rows_of(lo, 2 * CH) - odd24, values, values]
            )
        add_part(0, g)

    def store_grid(n):
        for s in range(n * SPLIT, (n + 1) * SPLIT):
            cols = slice((s - n * SPLIT) * send_cols, (s - n * SPLIT + 1) * send_cols)
            grid[s] = acc[:, cols].reshape(nb, LAT, send_cols).astype(BF16)
            pltpu.make_async_copy(grid.at[s, me], r2.at[s, me], recv2.at[s]).start()

    def send_grid(s, i):
        to = peer(i)
        pltpu.make_async_remote_copy(
            src_ref=grid.at[s, to], dst_ref=r2.at[s, me],
            send_sem=send2.at[s], recv_sem=recv2.at[s],
            device_id={"band": to}, device_id_type=MESH,
        ).start()

    steps = groups // SPLIT
    each = nb // steps

    def scatter(n, split):
        s = (n - 1) * SPLIT + split

        @pl.loop(0, steps)
        def _(g):
            @pl.when(g > 0)
            def _():
                send_grid(s, g * each)

            for k in range(1, each):
                send_grid(s, g * each + k)
            add_part(n, split * steps + g)

    def transform(n):
        pltpu.make_async_copy(grid.at[n], r2.at[n], recv2.at[n]).wait()
        nodes = r2[n].astype(F32).reshape(nb * LAT, send_cols).astype(BF16)
        modes = lax.dot_general(
            nodes, dct[...], (((0,), (0,)), ((), ())), preferred_element_type=F32
        )
        spec[lev, n * send_cols : (n + 1) * send_cols, :] = modes.astype(BF16)

    rows = CH * LON // PIECES

    def piece(level, i):
        return spec.at[level, i * rows : (i + 1) * rows]

    def push(level, i, to, sem):
        pltpu.make_async_remote_copy(
            src_ref=piece(level, i), dst_ref=piece(level, i),
            send_sem=send3, recv_sem=sem.at[i],
            device_id={"lev": to}, device_id_type=MESH,
        ).start()

    def arrived(level, i, sem):
        pltpu.make_async_copy(piece(level, i), piece(level, i), sem.at[i]).wait()

    def own(i):
        push(lev, i, right, recv_l)
        push(lev, i, left, recv_r)

    def relay(i):
        if i % 2 == 0:
            arrived(left, i, recv_l)
            push(left, i, right, recv_o)
        else:
            arrived(right, i, recv_r)
            push(right, i, left, recv_o)

    def encode(p):
        first = pl.multiple_of(p * 2 * CH, 2 * CH)
        span = spec.shape[2] // STRIPS
        for strip in range(STRIPS):
            cols = slice(strip * span, (strip + 1) * span)
            wide = spec[:, pl.ds(first, 2 * CH), cols].astype(F32)
            square = jnp.sum(wide * wide, axis=0)
            norms = []
            for par in range(2):
                mean = jnp.sum(square[par * CH : (par + 1) * CH], axis=0, keepdims=True)
                norms.append(rows_of(lax.rsqrt(mean * (1.0 / (ny * CH)) + EPS), CH))
            scale = jnp.concatenate(norms, 0)
            normed = [(wide[l] * scale).astype(BF16) for l in range(ny)]
            normed.append(jnp.ones((16, span), BF16))
            pre[strip] = jnp.dot(
                w1[...], jnp.concatenate(normed, 0), preferred_element_type=F32
            )
        for strip in range(STRIPS):
            cols = slice(strip * span, (strip + 1) * span)
            for par in range(2):
                act = []
                for r in range(0, hid, ROWS):
                    z = pre[strip, par * hid + r : par * hid + r + ROWS, :]
                    bend = jnp.tanh(z * (0.7978845608028654 + 0.035677408136300125 * (z * z)))
                    act.append((z + z * bend).astype(BF16))
                stage[:, 2 * p + par, cols] = (
                    jnp.dot(w2[...], jnp.concatenate(act), preferred_element_type=F32) + bias2[...]
                )

    ready = [(i + 1) * rows // (2 * CH) for i in range(PIECES)]

    def encode_pieces(first, last):
        for i in range(first, last):
            if i % 2 == 0:
                arrived(right, i, recv_r)
            else:
                arrived(left, i, recv_l)
            arrived(opp, i, recv_o)
        before, after = ready[first - 1] if first else 0, ready[last - 1]

        @pl.loop(before, after)
        def _(p):
            encode(p)

        lo_m, hi_m = before * 2 // 8 * 8, after * 2 // 8 * 8
        if hi_m > lo_m:
            out[:, lo_m:hi_m, :] = stage[:, lo_m:hi_m, :].astype(BF16)

    def launch(n):
        transform(n)
        own(2 * n)
        own(2 * n + 1)

    store_grid(0)
    acc[...] = clear
    scatter(1, 0)
    scatter(1, 1)
    store_grid(1)
    acc[...] = clear
    scatter(2, 0)
    launch(0)
    scatter(2, 1)
    launch(1)
    store_grid(2)

    @pl.loop(1, nb)
    def _(i):
        send_grid(2 * SPLIT, i)

    relay(0)
    relay(1)

    @pl.loop(1, nb)
    def _(i):
        send_grid(2 * SPLIT + 1, i)

    launch(2)
    launch(3)
    for i in range(2, 6):
        relay(i)
    launch(4)
    relay(6)
    relay(7)
    launch(5)
    encode_pieces(0, 2)
    encode_pieces(2, 4)
    relay(8)
    relay(9)
    encode_pieces(4, 6)
    relay(10)
    relay(11)
    encode_pieces(6, 8)
    encode_pieces(8, 10)
    encode_pieces(10, 12)

    pltpu.make_async_copy(s1.at[pl.ds(0, nb - 1)], r1.at[pl.ds(0, nb - 1)], send1).wait()
    for h in range(PARTS * SPLIT):
        sent = grid.at[h, pl.ds(0, nb - 1)]
        pltpu.make_async_copy(sent, sent, send2.at[h]).wait()
    sent = spec.at[pl.ds(0, 3)]
    pltpu.make_async_copy(sent, sent, send3).wait()


def on_device(nb, ny, obs_vals, obs_colat, obs_lon, band_list, counts, w_in, b_in, w_out, b_out):
    obs = obs_vals.shape[2]
    modes = nb * LAT
    outs = w_out.shape[1]
    part_cols = CH * LON // PARTS
    send_cols = part_cols // SPLIT
    groups = nb // GROUP
    dma = pltpu.SemaphoreType.DMA
    vmem = pl.BlockSpec(memory_space=pltpu.VMEM)
    args = (
        obs_vals[0],
        obs_colat.reshape(obs // CAP, CAP),
        obs_lon.reshape(obs // CAP, CAP),
        band_list[0],
        counts,
        jnp.asarray(cheb_inverse().T),
        jnp.asarray(dct_columns(modes)).astype(BF16),
        w_in,
        b_in[None, :],
        w_out.T,
        b_out[None, :],
    )
    return pl.pallas_call(
        functools.partial(kernel, nb, ny),
        out_shape=jax.ShapeDtypeStruct((outs, LON, modes), BF16),
        in_specs=[pl.BlockSpec(memory_space=pltpu.HBM)] * INPUTS,
        out_specs=vmem,
        scratch_shapes=[
            *(pltpu.VMEM(arg.shape, arg.dtype) for arg in args),
            pltpu.VMEM((nb, 1), F32),
            pltpu.VMEM((outs, 1), F32),
            pltpu.VMEM((obs // LANES * AUX, LANES), BF16),
            pltpu.VMEM((nb, AUX, CAP), BF16),
            pltpu.VMEM((nb, AUX, CAP), BF16),
            pltpu.VMEM((nb, 4 * LAT + 4 * CH, CAP), F32),
            pltpu.VMEM((nb * LAT, part_cols), F32),
            pltpu.VMEM((PARTS * SPLIT, nb, LAT, send_cols), BF16),
            pltpu.VMEM((PARTS * SPLIT, nb, LAT, send_cols), BF16),
            pltpu.VMEM((ny, LON * CH, modes), BF16),
            pltpu.VMEM((2 * w_in.shape[1], 2 * w_in.shape[0] + 16), BF16),
            pltpu.VMEM((outs, w_out.shape[0]), BF16),
            pltpu.VMEM((STRIPS, 2 * w_in.shape[1], modes // STRIPS), F32),
            pltpu.VMEM((outs, LON, modes), F32),
            dma((INPUTS,)), dma, dma((groups,)), dma((PARTS * SPLIT,)), dma((PARTS * SPLIT,)),
            dma, dma((PIECES,)), dma((PIECES,)), dma((PIECES,)),
        ],
        compiler_params=pltpu.CompilerParams(
            collective_id=0, has_side_effects=True, vmem_limit_bytes=40 * 1024 * 1024
        ),
    )(*(pltpu.with_memory_space_constraint(arg, pltpu.HBM) for arg in args))


def solution(mesh):
    nb, ny = mesh.shape["band"], mesh.shape["lev"]
    in_specs = (
        P("lev", None, "band"),
        P("band"),
        P("band"),
        P("band", None, None),
        P("band", None),
        P(),
        P(),
        P(None, "lev"),
        P("lev"),
    )
    return jax.shard_map(
        functools.partial(on_device, nb, ny),
        mesh=mesh, in_specs=in_specs, out_specs=P("lev", "band", None), check_vma=False,
    )
```

```python
import functools
import math

import jax
import jax.numpy as jnp
import numpy as np
from jax import lax
from jax.experimental import pallas as pl
from jax.experimental.pallas import tpu as pltpu
from jax.sharding import PartitionSpec as P

LAT = 8
LON = 32
CH = 24
CAP = 128
AUX = 32
LANES = 256
INPUTS = 11
GROUP = 8
DEPTHS, CORES = 8, 2
PARTS = 3
SPLIT = 2
DEPTH = 8
PIECES = 12
STRIPS = 1
ROWS = 16
EPS = 1e-05
F32, BF16, I32 = jnp.float32, jnp.bfloat16, jnp.int32
MESH = pl.DeviceIdType.MESH


def cheb_inverse():
    order = np.arange(LAT, dtype=np.float64)[:, None]
    node = np.arange(LAT, dtype=np.float64)[None, :]
    factor = np.where(order == 0.0, 1.0, 2.0) / LAT
    return (factor * np.cos(math.pi * order * (node + 0.5) / LAT)).astype(np.float32)


def dct_columns(length):
    mode = np.arange(length, dtype=np.float64)[None, :]
    node = np.arange(length, dtype=np.float64)[:, None]
    scale = np.where(mode == 0.0, math.sqrt(1.0 / length), math.sqrt(2.0 / length))
    return (scale * np.cos(math.pi * mode * (node + 0.5) / length)).astype(np.float32)


def rows_of(value, rows):
    return jnp.broadcast_to(value, (rows, value.shape[1]))


def kernel(
    nb, ny,
    *refs,
):
    hbm, out, local = refs[:INPUTS], refs[INPUTS], refs[INPUTS + 1 : 2 * INPUTS + 1]
    vals, colat, lon, bl, cnt, inv_tab, dct, w_in, b_in, w_out, b_out = local
    (
        live_n, bias2, table, s1, r1, prep, acc, grid, r2, spec, w1, w2, pre, stage,
        load, send1, recv1, send2, recv2, send3, recv_l, recv_r, recv_o,
    ) = refs[2 * INPUTS + 1 :]
    me = lax.axis_index("band")
    lev = lax.axis_index("lev")
    right = lax.rem(lev + 1, ny)
    left = lax.rem(lev + ny - 1, ny)
    opp = lax.rem(lev + 2, ny)
    part_cols = CH * LON // PARTS
    send_cols = part_cols // SPLIT
    groups = nb // GROUP
    hid = b_in.shape[1]

    wide_x = nb // (DEPTHS * CORES)
    my_x, my_z, my_core = me // (DEPTHS * CORES), lax.rem(me // CORES, DEPTHS), lax.rem(me, CORES)

    def far_first(j, size):
        return size // 2 + (j + 1) // 2 * (1 - 2 * (j % 2))

    in_plane = [
        lax.rem(my_x + far_first(j // CORES, wide_x), wide_x) * (DEPTHS * CORES)
        + lax.rem(my_core + CORES - 1 - j % CORES, CORES)
        for j in range(GROUP)
    ]

    def along_z(k):
        step = DEPTHS // 2 + (k + 1) // 2 * (1 - 2 * lax.rem(k, 2))
        return lax.rem(my_z + step, DEPTHS) * CORES

    def unless_own(j, other, do):
        if j < GROUP - 1:
            do()
        else:
            pl.when(other)(do)

    loads = [pltpu.make_async_copy(hbm[k], local[k], load.at[k]) for k in range(INPUTS)]
    for copy in loads:
        copy.start()
    barrier = pltpu.get_barrier_semaphore()

    @pl.loop(0, groups)
    def _(k):
        z = along_z(k)
        for j in range(GROUP):
            unless_own(
                j, k < groups - 1,
                lambda j=j: pl.semaphore_signal(
                    barrier, inc=1, device_id={"band": in_plane[j] + z}, device_id_type=MESH
                ),
            )

    for y in (left, right):
        pl.semaphore_signal(barrier, inc=1, device_id={"lev": y}, device_id_type=MESH)

    for copy in loads:
        copy.wait()
    for row, column in ((cnt, live_n), (b_out, bias2)):
        n, copies = row.shape[1], column.shape[1]
        r_id = lax.broadcasted_iota(I32, (n, n), 0)
        c_id = lax.broadcasted_iota(I32, (n, n), 1)
        wide_row = rows_of(row[...].astype(F32), n)
        one = jnp.sum(jnp.where(r_id == c_id, wide_row, 0.0), axis=1, keepdims=True)
        column[...] = jnp.broadcast_to(one, (n, copies))

    obs = vals.shape[1]
    pieces = obs // LANES
    lon_v = lon[...]
    lon_hi, lon_lo = (lon_v // LON).astype(F32), (lon_v % LON).astype(F32)
    pos = colat[...].astype(F32)
    row8 = lax.broadcasted_iota(I32, (8, CAP), 0)
    for h in range(pieces):
        table[h * AUX : h * AUX + CH, :] = vals[:, h * LANES : (h + 1) * LANES]
        for part in range(LANES // CAP):
            r = h * (LANES // CAP) + part
            aux = jnp.zeros((8, CAP), F32)
            for k, source in enumerate((pos, lon_hi, lon_lo)):
                aux = jnp.where(row8 == k, rows_of(source[r : r + 1], 8), aux)
            table[h * AUX + CH : (h + 1) * AUX, part * CAP : (part + 1) * CAP] = aux.astype(BF16)

    batch = 4
    lane = lax.broadcasted_iota(I32, (1, CAP), 1)
    sub = lax.broadcasted_iota(I32, (LANES, CAP), 0)

    def sort_batch(k, first):
        hots, his = [], []
        for j in range(first, first + batch):
            b = in_plane[j] + along_z(k)
            idx = bl[pl.ds(b, 1), :]
            live = lane.astype(F32) < live_n[pl.ds(b, 1), :]
            his.append(jnp.where(live, idx // LANES, -1))
            hots.append(jnp.where(sub == rows_of(idx % LANES, LANES), 1.0, 0.0).astype(BF16))
        picked = jnp.dot(table[...], jnp.concatenate(hots, 1), preferred_element_type=F32)
        hi = rows_of(jnp.concatenate(his, 1), AUX)
        block = jnp.zeros((AUX, batch * CAP), F32)
        for h in range(pieces):
            block = jnp.where(hi == h, picked[h * AUX : (h + 1) * AUX], block)
        block = block.astype(BF16)
        for u in range(batch):
            s1[k * GROUP + first + u] = block[:, u * CAP : (u + 1) * CAP]

    def send_block(k, j):
        i = k * GROUP + j

        def go():
            pltpu.make_async_remote_copy(
                src_ref=s1.at[i], dst_ref=r1.at[i],
                send_sem=send1, recv_sem=recv1.at[k],
                device_id={"band": in_plane[j] + along_z(k)}, device_id_type=MESH,
            ).start()

        unless_own(j, k < groups - 1, go)

    early = groups * 3 // 4

    @pl.loop(0, early)
    def _(k):
        for first in range(0, GROUP, batch):
            sort_batch(k, first)

    pl.semaphore_wait(barrier, nb - 1 + 2)

    @pl.loop(0, early)
    def _(k):
        for j in range(GROUP):
            send_block(k, j)

    @pl.loop(early, groups)
    def _(k):
        for first in range(0, GROUP, batch):
            sort_batch(k, first)
            for j in range(first, first + batch):
                send_block(k, j)

    pltpu.make_async_copy(s1.at[nb - 1], r1.at[nb - 1], recv1.at[groups - 1]).start()

    zero = jnp.zeros((CH, hid), F32)
    stacked = []
    for l in range(ny):
        w_l = w_in[l * CH : (l + 1) * CH, :].astype(F32)
        stacked.append(jnp.concatenate([w_l, zero], 1))
        stacked.append(jnp.concatenate([zero, w_l], 1))
    bias = jnp.concatenate([b_in[...]] * 2, 1)
    coarse = bias.astype(BF16).astype(F32)
    row16 = lax.broadcasted_iota(I32, (16, 2 * hid), 0)
    stacked.append(
        jnp.where(row16 == 0, rows_of(coarse, 16), jnp.where(row16 == 1, rows_of(bias - coarse, 16), 0.0))
    )
    w1[...] = jnp.concatenate(stacked, 0).T.astype(BF16)
    w2[...] = (0.5 * w_out[...].astype(F32)).astype(BF16)

    odd8 = (lax.broadcasted_iota(I32, (2 * LAT, CAP), 0) // LAT).astype(F32)
    odd24 = (lax.broadcasted_iota(I32, (2 * CH, CAP), 0) // CH).astype(F32)
    nt = (((1,), (1,)), ((), ()))

    def add_part(n, g):
        total = None
        for first in range(0, GROUP, DEPTH):
            lefts, rights = [], []
            for t in range(first, first + DEPTH):
                block = prep[g * GROUP + t].astype(BF16)
                hi_two, w_two = block[0 : 2 * LAT], block[2 * LAT : 4 * LAT]
                none = jnp.zeros_like(w_two)
                lefts.append(
                    jnp.concatenate(
                        [
                            jnp.where(hi_two == jnp.asarray(2.0 * q, BF16), w_two, none)
                            for q in range(nb // 2)
                        ]
                    )
                )
                tiles = []
                for tile in range(n * part_cols // 16, (n + 1) * part_cols // 16):
                    q, third = divmod(tile, 3)
                    at = 4 * LAT + 16 * third
                    tiles.append(
                        jnp.where(
                            block[at : at + 16] == jnp.asarray(2.0 * q, BF16),
                            block[at + 2 * CH : at + 2 * CH + 16],
                            none,
                        )
                    )
                rights.append(jnp.concatenate(tiles))
            term = lax.dot_general(
                jnp.concatenate(lefts, 1), jnp.concatenate(rights, 1), nt,
                preferred_element_type=F32,
            )
            total = term if total is None else total + term
        acc[...] += total

    clear = jnp.zeros(acc.shape, F32)
    columns = [jnp.broadcast_to(inv_tab[:, k : k + 1], (LAT, CAP)) for k in range(LAT)]
    acc[...] = clear

    @pl.loop(0, groups)
    def _(turn):
        g = lax.rem(turn + groups - 1, groups)
        pltpu.make_async_copy(
            s1.at[pl.ds(0, GROUP)], r1.at[pl.ds(0, GROUP)], recv1.at[g]
        ).wait()
        for t in range(GROUP):
            got = r1[g * GROUP + t]
            tail = got[CH:AUX].astype(F32)
            x, hi, lo = tail[0:1], tail[1:2], tail[2:3]
            weight = columns[0] + columns[1] * x
            t_prev, t_now = jnp.ones_like(x), x
            for k in range(2, LAT):
                t_prev, t_now = t_now, 2.0 * x * t_now - t_prev
                weight = weight + columns[k] * t_now
            values = got[0:CH].astype(F32)
            prep[g * GROUP + t] = jnp.concatenate(
                [rows_of(hi, 2 * LAT) - odd8, weight, weight, rows_of(lo, 2 * CH) - odd24, values, values]
            )
        add_part(0, g)

    def store_grid(n):
        for s in range(n * SPLIT, (n + 1) * SPLIT):
            cols = slice((s - n * SPLIT) * send_cols, (s - n * SPLIT + 1) * send_cols)
            grid[s] = acc[:, cols].reshape(nb, LAT, send_cols).astype(BF16)
            pltpu.make_async_copy(grid.at[s, me], r2.at[s, me], recv2.at[s]).start()

    def send_grid(s, k):
        z = along_z(k)
        for j in range(GROUP):

            def go(to=in_plane[j] + z):
                pltpu.make_async_remote_copy(
                    src_ref=grid.at[s, to], dst_ref=r2.at[s, me],
                    send_sem=send2.at[s], recv_sem=recv2.at[s],
                    device_id={"band": to}, device_id_type=MESH,
                ).start()

            unless_own(j, k < groups - 1, go)

    steps = groups // SPLIT

    def scatter(n, split, first, last):
        s = (n - 1) * SPLIT + split

        @pl.loop(first, last)
        def _(g):
            for k in range(SPLIT):
                send_grid(s, g * SPLIT + k)
            add_part(n, split * steps + g)

    def transform(n):
        pltpu.make_async_copy(grid.at[n], r2.at[n], recv2.at[n]).wait()
        nodes = r2[n].astype(F32).reshape(nb * LAT, send_cols).astype(BF16)
        modes = lax.dot_general(
            nodes, dct[...], (((0,), (0,)), ((), ())), preferred_element_type=F32
        )
        spec[lev, n * send_cols : (n + 1) * send_cols, :] = modes.astype(BF16)

    rows = CH * LON // PIECES

    def piece(level, i):
        return spec.at[level, i * rows : (i + 1) * rows]

    def push(level, i, to, sem):
        pltpu.make_async_remote_copy(
            src_ref=piece(level, i), dst_ref=piece(level, i),
            send_sem=send3, recv_sem=sem.at[i],
            device_id={"lev": to}, device_id_type=MESH,
        ).start()

    def arrived(level, i, sem):
        pltpu.make_async_copy(piece(level, i), piece(level, i), sem.at[i]).wait()

    def relay(i):
        if i % 2 == 0:
            arrived(left, i, recv_l)
            push(left, i, right, recv_o)
        else:
            arrived(right, i, recv_r)
            push(right, i, left, recv_o)

    def encode(p):
        first = pl.multiple_of(p * 2 * CH, 2 * CH)
        span = spec.shape[2] // STRIPS
        for strip in range(STRIPS):
            cols = slice(strip * span, (strip + 1) * span)
            wide = spec[:, pl.ds(first, 2 * CH), cols].astype(F32)
            square = jnp.sum(wide * wide, axis=0)
            norms = []
            for par in range(2):
                mean = jnp.sum(square[par * CH : (par + 1) * CH], axis=0, keepdims=True)
                norms.append(rows_of(lax.rsqrt(mean * (1.0 / (ny * CH)) + EPS), CH))
            scale = jnp.concatenate(norms, 0)
            normed = [(wide[l] * scale).astype(BF16) for l in range(ny)]
            normed.append(jnp.ones((16, span), BF16))
            pre[strip] = jnp.dot(
                w1[...], jnp.concatenate(normed, 0), preferred_element_type=F32
            )
        for strip in range(STRIPS):
            cols = slice(strip * span, (strip + 1) * span)
            for par in range(2):
                act = []
                for r in range(0, hid, ROWS):
                    z = pre[strip, par * hid + r : par * hid + r + ROWS, :]
                    bend = jnp.tanh(z * (0.7978845608028654 + 0.035677408136300125 * (z * z)))
                    act.append((z + z * bend).astype(BF16))
                stage[:, 2 * p + par, cols] = (
                    jnp.dot(w2[...], jnp.concatenate(act), preferred_element_type=F32) + bias2[...]
                )

    ready = [(i + 1) * rows // (2 * CH) for i in range(PIECES)]

    def encode_pieces(first, last):
        for i in range(first, last):
            if i % 2 == 0:
                arrived(right, i, recv_r)
            else:
                arrived(left, i, recv_l)
            arrived(opp, i, recv_o)
        before, after = ready[first - 1] if first else 0, ready[last - 1]

        @pl.loop(before, after)
        def _(p):
            encode(p)

        lo_m, hi_m = before * 2 // 8 * 8, after * 2 // 8 * 8
        if hi_m > lo_m:
            out[:, lo_m:hi_m, :] = stage[:, lo_m:hi_m, :].astype(BF16)

    def launch(n):
        transform(n)
        push(lev, 2 * n, right, recv_l)
        push(lev, 2 * n + 1, left, recv_r)
        push(lev, 2 * n, left, recv_r)
        push(lev, 2 * n + 1, right, recv_l)

    store_grid(0)
    acc[...] = clear
    scatter(1, 0, 0, steps)
    scatter(1, 1, 0, steps)
    store_grid(1)
    acc[...] = clear
    scatter(2, 0, 0, steps // 2)
    launch(0)
    scatter(2, 0, steps // 2, steps)
    scatter(2, 1, 0, steps // 2)
    launch(1)
    scatter(2, 1, steps // 2, steps)
    store_grid(2)

    @pl.loop(0, groups)
    def _(k):
        send_grid(2 * SPLIT, k)

    relay(0)
    relay(1)

    @pl.loop(0, groups)
    def _(k):
        send_grid(2 * SPLIT + 1, k)

    launch(2)
    launch(3)
    for i in range(2, 6):
        relay(i)
    launch(4)
    relay(6)
    relay(7)
    launch(5)
    encode_pieces(0, 2)
    encode_pieces(2, 4)
    relay(8)
    relay(9)
    encode_pieces(4, 6)
    relay(10)
    relay(11)
    encode_pieces(6, 8)
    encode_pieces(8, 10)
    encode_pieces(10, 12)

    pltpu.make_async_copy(s1.at[pl.ds(0, nb - 1)], r1.at[pl.ds(0, nb - 1)], send1).wait()
    for h in range(PARTS * SPLIT):
        sent = grid.at[h, pl.ds(0, nb - 1)]
        pltpu.make_async_copy(sent, sent, send2.at[h]).wait()
    sent = spec.at[pl.ds(0, 3)]
    pltpu.make_async_copy(sent, sent, send3).wait()


def on_device(nb, ny, obs_vals, obs_colat, obs_lon, band_list, counts, w_in, b_in, w_out, b_out):
    obs = obs_vals.shape[2]
    modes = nb * LAT
    outs = w_out.shape[1]
    part_cols = CH * LON // PARTS
    send_cols = part_cols // SPLIT
    groups = nb // GROUP
    dma = pltpu.SemaphoreType.DMA
    vmem = pl.BlockSpec(memory_space=pltpu.VMEM)
    args = (
        obs_vals[0],
        obs_colat.reshape(obs // CAP, CAP),
        obs_lon.reshape(obs // CAP, CAP),
        band_list[0],
        counts,
        jnp.asarray(cheb_inverse().T),
        jnp.asarray(dct_columns(modes)).astype(BF16),
        w_in,
        b_in[None, :],
        w_out.T,
        b_out[None, :],
    )
    return pl.pallas_call(
        functools.partial(kernel, nb, ny),
        out_shape=jax.ShapeDtypeStruct((outs, LON, modes), BF16),
        in_specs=[pl.BlockSpec(memory_space=pltpu.HBM)] * INPUTS,
        out_specs=vmem,
        scratch_shapes=[
            *(pltpu.VMEM(arg.shape, arg.dtype) for arg in args),
            pltpu.VMEM((nb, 1), F32),
            pltpu.VMEM((outs, 1), F32),
            pltpu.VMEM((obs // LANES * AUX, LANES), BF16),
            pltpu.VMEM((nb, AUX, CAP), BF16),
            pltpu.VMEM((nb, AUX, CAP), BF16),
            pltpu.VMEM((nb, 4 * LAT + 4 * CH, CAP), F32),
            pltpu.VMEM((nb * LAT, part_cols), F32),
            pltpu.VMEM((PARTS * SPLIT, nb, LAT, send_cols), BF16),
            pltpu.VMEM((PARTS * SPLIT, nb, LAT, send_cols), BF16),
            pltpu.VMEM((ny, LON * CH, modes), BF16),
            pltpu.VMEM((2 * w_in.shape[1], 2 * w_in.shape[0] + 16), BF16),
            pltpu.VMEM((outs, w_out.shape[0]), BF16),
            pltpu.VMEM((STRIPS, 2 * w_in.shape[1], modes // STRIPS), F32),
            pltpu.VMEM((outs, LON, modes), F32),
            dma((INPUTS,)), dma, dma((groups,)), dma((PARTS * SPLIT,)), dma((PARTS * SPLIT,)),
            dma, dma((PIECES,)), dma((PIECES,)), dma((PIECES,)),
        ],
        compiler_params=pltpu.CompilerParams(
            collective_id=0, has_side_effects=True, vmem_limit_bytes=40 * 1024 * 1024
        ),
    )(*(pltpu.with_memory_space_constraint(arg, pltpu.HBM) for arg in args))


def solution(mesh):
    nb, ny = mesh.shape["band"], mesh.shape["lev"]
    in_specs = (
        P("lev", None, "band"),
        P("band"),
        P("band"),
        P("band", None, None),
        P("band", None),
        P(),
        P(),
        P(None, "lev"),
        P("lev"),
    )
    return jax.shard_map(
        functools.partial(on_device, nb, ny),
        mesh=mesh, in_specs=in_specs, out_specs=P("lev", "band", None), check_vma=False,
    )
```

```python
import functools
import math

import jax
import jax.numpy as jnp
import numpy as np
from jax import lax
from jax.experimental import pallas as pl
from jax.experimental.pallas import tpu as pltpu
from jax.sharding import PartitionSpec as P

LAT = 8
LON = 32
CH = 24
CAP = 128
AUX = 32
LANES = 256
INPUTS = 11
GROUP = 8
DEPTHS, CORES = 8, 2
PARTS = 3
SPLIT = 2
DEPTH = 8
PIECES = 12
STRIPS = 1
ROWS = 16
EPS = 1e-05
F32, BF16, I32 = jnp.float32, jnp.bfloat16, jnp.int32
MESH = pl.DeviceIdType.MESH


def cheb_inverse():
    order = np.arange(LAT, dtype=np.float64)[:, None]
    node = np.arange(LAT, dtype=np.float64)[None, :]
    factor = np.where(order == 0.0, 1.0, 2.0) / LAT
    return (factor * np.cos(math.pi * order * (node + 0.5) / LAT)).astype(np.float32)


def dct_columns(length):
    mode = np.arange(length, dtype=np.float64)[None, :]
    node = np.arange(length, dtype=np.float64)[:, None]
    scale = np.where(mode == 0.0, math.sqrt(1.0 / length), math.sqrt(2.0 / length))
    return (scale * np.cos(math.pi * mode * (node + 0.5) / length)).astype(np.float32)


def rows_of(value, rows):
    return jnp.broadcast_to(value, (rows, value.shape[1]))


def kernel(
    nb, ny,
    *refs,
):
    hbm, out, local = refs[:INPUTS], refs[INPUTS], refs[INPUTS + 1 : 2 * INPUTS + 1]
    vals, colat, lon, bl, cnt, inv_tab, dct, w_in, b_in, w_out, b_out = local
    (
        live_n, bias2, table, s1, r1, prep, acc, grid, r2, spec, w1, w2, pre, stage,
        load, send1, recv1, send2, recv2, send3, recv_l, recv_r, recv_o,
    ) = refs[2 * INPUTS + 1 :]
    me = lax.axis_index("band")
    lev = lax.axis_index("lev")
    right = lax.rem(lev + 1, ny)
    left = lax.rem(lev + ny - 1, ny)
    opp = lax.rem(lev + 2, ny)
    part_cols = CH * LON // PARTS
    send_cols = part_cols // SPLIT
    groups = nb // GROUP
    hid = b_in.shape[1]

    wide_x = nb // (DEPTHS * CORES)
    my_x, my_z, my_core = me // (DEPTHS * CORES), lax.rem(me // CORES, DEPTHS), lax.rem(me, CORES)

    def far_first(j, size):
        return size // 2 + (j + 1) // 2 * (1 - 2 * (j % 2))

    in_plane = [
        lax.rem(my_x + far_first(j // CORES, wide_x), wide_x) * (DEPTHS * CORES)
        + lax.rem(my_core + CORES - 1 - j % CORES, CORES)
        for j in range(GROUP)
    ]

    def along_z(k):
        step = DEPTHS // 2 + (k + 1) // 2 * (1 - 2 * lax.rem(k, 2))
        return lax.rem(my_z + step, DEPTHS) * CORES

    def unless_own(j, other, do):
        if j < GROUP - 1:
            do()
        else:
            pl.when(other)(do)

    loads = [pltpu.make_async_copy(hbm[k], local[k], load.at[k]) for k in range(INPUTS)]
    for copy in loads:
        copy.start()
    barrier = pltpu.get_barrier_semaphore()

    @pl.loop(0, groups)
    def _(k):
        z = along_z(k)
        for j in range(GROUP):
            unless_own(
                j, k < groups - 1,
                lambda j=j: pl.semaphore_signal(
                    barrier, inc=1, device_id={"band": in_plane[j] + z}, device_id_type=MESH
                ),
            )

    for y in (left, right):
        pl.semaphore_signal(barrier, inc=1, device_id={"lev": y}, device_id_type=MESH)

    for copy in loads:
        copy.wait()
    for row, column in ((cnt, live_n), (b_out, bias2)):
        n, copies = row.shape[1], column.shape[1]
        r_id = lax.broadcasted_iota(I32, (n, n), 0)
        c_id = lax.broadcasted_iota(I32, (n, n), 1)
        wide_row = rows_of(row[...].astype(F32), n)
        one = jnp.sum(jnp.where(r_id == c_id, wide_row, 0.0), axis=1, keepdims=True)
        column[...] = jnp.broadcast_to(one, (n, copies))

    obs = vals.shape[1]
    pieces = obs // LANES
    lon_v = lon[...]
    lon_hi, lon_lo = (lon_v // LON).astype(F32), (lon_v % LON).astype(F32)
    pos = colat[...].astype(F32)
    row8 = lax.broadcasted_iota(I32, (8, CAP), 0)
    for h in range(pieces):
        table[h * AUX : h * AUX + CH, :] = vals[:, h * LANES : (h + 1) * LANES]
        for part in range(LANES // CAP):
            r = h * (LANES // CAP) + part
            aux = jnp.zeros((8, CAP), F32)
            for k, source in enumerate((pos, lon_hi, lon_lo)):
                aux = jnp.where(row8 == k, rows_of(source[r : r + 1], 8), aux)
            table[h * AUX + CH : (h + 1) * AUX, part * CAP : (part + 1) * CAP] = aux.astype(BF16)

    batch = 4
    lane = lax.broadcasted_iota(I32, (1, CAP), 1)
    sub = lax.broadcasted_iota(I32, (LANES, CAP), 0)

    def sort_batch(k, first):
        hots, his = [], []
        for j in range(first, first + batch):
            b = in_plane[j] + along_z(k)
            idx = bl[pl.ds(b, 1), :]
            live = lane.astype(F32) < live_n[pl.ds(b, 1), :]
            his.append(jnp.where(live, idx // LANES, -1))
            hots.append(jnp.where(sub == rows_of(idx % LANES, LANES), 1.0, 0.0).astype(BF16))
        picked = jnp.dot(table[...], jnp.concatenate(hots, 1), preferred_element_type=F32)
        hi = rows_of(jnp.concatenate(his, 1), AUX)
        block = jnp.zeros((AUX, batch * CAP), F32)
        for h in range(pieces):
            block = jnp.where(hi == h, picked[h * AUX : (h + 1) * AUX], block)
        block = block.astype(BF16)
        for u in range(batch):
            s1[k * GROUP + first + u] = block[:, u * CAP : (u + 1) * CAP]

    def send_block(k, j):
        i = k * GROUP + j

        def go():
            pltpu.make_async_remote_copy(
                src_ref=s1.at[i], dst_ref=r1.at[i],
                send_sem=send1, recv_sem=recv1.at[k],
                device_id={"band": in_plane[j] + along_z(k)}, device_id_type=MESH,
            ).start()

        unless_own(j, k < groups - 1, go)

    early = groups // 2

    @pl.loop(0, early)
    def _(k):
        for first in range(0, GROUP, batch):
            sort_batch(k, first)

    pl.semaphore_wait(barrier, nb - 1 + 2)

    @pl.loop(0, early)
    def _(k):
        for j in range(GROUP):
            send_block(k, j)

    @pl.loop(early, groups)
    def _(k):
        for first in range(0, GROUP, batch):
            sort_batch(k, first)
            for j in range(first, first + batch):
                send_block(k, j)

    pltpu.make_async_copy(s1.at[nb - 1], r1.at[nb - 1], recv1.at[groups - 1]).start()

    zero = jnp.zeros((CH, hid), F32)
    stacked = []
    for l in range(ny):
        w_l = w_in[l * CH : (l + 1) * CH, :].astype(F32)
        stacked.append(jnp.concatenate([w_l, zero], 1))
        stacked.append(jnp.concatenate([zero, w_l], 1))
    bias = jnp.concatenate([b_in[...]] * 2, 1)
    coarse = bias.astype(BF16).astype(F32)
    row16 = lax.broadcasted_iota(I32, (16, 2 * hid), 0)
    stacked.append(
        jnp.where(row16 == 0, rows_of(coarse, 16), jnp.where(row16 == 1, rows_of(bias - coarse, 16), 0.0))
    )
    w1[...] = jnp.concatenate(stacked, 0).T.astype(BF16)
    w2[...] = (0.5 * w_out[...].astype(F32)).astype(BF16)

    odd8 = (lax.broadcasted_iota(I32, (2 * LAT, CAP), 0) // LAT).astype(F32)
    odd24 = (lax.broadcasted_iota(I32, (2 * CH, CAP), 0) // CH).astype(F32)
    nt = (((1,), (1,)), ((), ()))

    def add_part(n, g):
        total = None
        for first in range(0, GROUP, DEPTH):
            lefts, rights = [], []
            for t in range(first, first + DEPTH):
                block = prep[g * GROUP + t].astype(BF16)
                hi_two, w_two = block[0 : 2 * LAT], block[2 * LAT : 4 * LAT]
                none = jnp.zeros_like(w_two)
                lefts.append(
                    jnp.concatenate(
                        [
                            jnp.where(hi_two == jnp.asarray(2.0 * q, BF16), w_two, none)
                            for q in range(nb // 2)
                        ]
                    )
                )
                tiles = []
                for tile in range(n * part_cols // 16, (n + 1) * part_cols // 16):
                    q, third = divmod(tile, 3)
                    at = 4 * LAT + 16 * third
                    tiles.append(
                        jnp.where(
                            block[at : at + 16] == jnp.asarray(2.0 * q, BF16),
                            block[at + 2 * CH : at + 2 * CH + 16],
                            none,
                        )
                    )
                rights.append(jnp.concatenate(tiles))
            term = lax.dot_general(
                jnp.concatenate(lefts, 1), jnp.concatenate(rights, 1), nt,
                preferred_element_type=F32,
            )
            total = term if total is None else total + term
        acc[...] += total

    clear = jnp.zeros(acc.shape, F32)
    columns = [jnp.broadcast_to(inv_tab[:, k : k + 1], (LAT, CAP)) for k in range(LAT)]
    acc[...] = clear

    @pl.loop(0, groups)
    def _(turn):
        g = lax.rem(turn + groups - 1, groups)
        pltpu.make_async_copy(
            s1.at[pl.ds(0, GROUP)], r1.at[pl.ds(0, GROUP)], recv1.at[g]
        ).wait()
        for t in range(GROUP):
            got = r1[g * GROUP + t]
            tail = got[CH:AUX].astype(F32)
            x, hi, lo = tail[0:1], tail[1:2], tail[2:3]
            weight = columns[0] + columns[1] * x
            t_prev, t_now = jnp.ones_like(x), x
            for k in range(2, LAT):
                t_prev, t_now = t_now, 2.0 * x * t_now - t_prev
                weight = weight + columns[k] * t_now
            values = got[0:CH].astype(F32)
            prep[g * GROUP + t] = jnp.concatenate(
                [rows_of(hi, 2 * LAT) - odd8, weight, weight, rows_of(lo, 2 * CH) - odd24, values, values]
            )
        add_part(0, g)

    def store_grid(n):
        for s in range(n * SPLIT, (n + 1) * SPLIT):
            cols = slice((s - n * SPLIT) * send_cols, (s - n * SPLIT + 1) * send_cols)
            grid[s] = acc[:, cols].reshape(nb, LAT, send_cols).astype(BF16)
            pltpu.make_async_copy(grid.at[s, me], r2.at[s, me], recv2.at[s]).start()

    def send_grid(s, k):
        z = along_z(k)
        for j in range(GROUP):

            def go(to=in_plane[j] + z):
                pltpu.make_async_remote_copy(
                    src_ref=grid.at[s, to], dst_ref=r2.at[s, me],
                    send_sem=send2.at[s], recv_sem=recv2.at[s],
                    device_id={"band": to}, device_id_type=MESH,
                ).start()

            unless_own(j, k < groups - 1, go)

    steps = groups // SPLIT

    def scatter(n, split, first, last):
        s = (n - 1) * SPLIT + split

        @pl.loop(first, last)
        def _(g):
            for k in range(SPLIT):
                send_grid(s, g * SPLIT + k)
            add_part(n, split * steps + g)

    def transform(n):
        pltpu.make_async_copy(grid.at[n], r2.at[n], recv2.at[n]).wait()
        nodes = r2[n].astype(F32).reshape(nb * LAT, send_cols).astype(BF16)
        modes = lax.dot_general(
            nodes, dct[...], (((0,), (0,)), ((), ())), preferred_element_type=F32
        )
        spec[lev, n * send_cols : (n + 1) * send_cols, :] = modes.astype(BF16)

    rows = CH * LON // PIECES

    def piece(level, i):
        return spec.at[level, i * rows : (i + 1) * rows]

    def push(level, i, to, sem):
        pltpu.make_async_remote_copy(
            src_ref=piece(level, i), dst_ref=piece(level, i),
            send_sem=send3, recv_sem=sem.at[i],
            device_id={"lev": to}, device_id_type=MESH,
        ).start()

    def arrived(level, i, sem):
        pltpu.make_async_copy(piece(level, i), piece(level, i), sem.at[i]).wait()

    def relay(i):
        if i % 2 == 0:
            arrived(left, i, recv_l)
            push(left, i, right, recv_o)
        else:
            arrived(right, i, recv_r)
            push(right, i, left, recv_o)

    def encode(p):
        first = pl.multiple_of(p * 2 * CH, 2 * CH)
        span = spec.shape[2] // STRIPS
        for strip in range(STRIPS):
            cols = slice(strip * span, (strip + 1) * span)
            wide = spec[:, pl.ds(first, 2 * CH), cols].astype(F32)
            square = jnp.sum(wide * wide, axis=0)
            norms = []
            for par in range(2):
                mean = jnp.sum(square[par * CH : (par + 1) * CH], axis=0, keepdims=True)
                norms.append(rows_of(lax.rsqrt(mean * (1.0 / (ny * CH)) + EPS), CH))
            scale = jnp.concatenate(norms, 0)
            normed = [(wide[l] * scale).astype(BF16) for l in range(ny)]
            normed.append(jnp.ones((16, span), BF16))
            pre[strip] = jnp.dot(
                w1[...], jnp.concatenate(normed, 0), preferred_element_type=F32
            )
        for strip in range(STRIPS):
            cols = slice(strip * span, (strip + 1) * span)
            for par in range(2):
                act = []
                for r in range(0, hid, ROWS):
                    z = pre[strip, par * hid + r : par * hid + r + ROWS, :]
                    bend = jnp.tanh(z * (0.7978845608028654 + 0.035677408136300125 * (z * z)))
                    act.append((z + z * bend).astype(BF16))
                stage[:, 2 * p + par, cols] = (
                    jnp.dot(w2[...], jnp.concatenate(act), preferred_element_type=F32) + bias2[...]
                )

    ready = [(i + 1) * rows // (2 * CH) for i in range(PIECES)]

    def encode_pieces(first, last):
        for i in range(first, last):
            if i % 2 == 0:
                arrived(right, i, recv_r)
            else:
                arrived(left, i, recv_l)
            arrived(opp, i, recv_o)
        before, after = ready[first - 1] if first else 0, ready[last - 1]

        @pl.loop(before, after)
        def _(p):
            encode(p)

        lo_m, hi_m = before * 2 // 8 * 8, after * 2 // 8 * 8
        if hi_m > lo_m:
            out[:, lo_m:hi_m, :] = stage[:, lo_m:hi_m, :].astype(BF16)

    def launch(n):
        transform(n)
        push(lev, 2 * n, right, recv_l)
        push(lev, 2 * n + 1, left, recv_r)
        push(lev, 2 * n, left, recv_r)
        push(lev, 2 * n + 1, right, recv_l)

    store_grid(0)
    acc[...] = clear
    scatter(1, 0, 0, steps)
    scatter(1, 1, 0, steps)
    store_grid(1)
    acc[...] = clear
    scatter(2, 0, 0, steps // 2)
    launch(0)
    scatter(2, 0, steps // 2, steps)
    scatter(2, 1, 0, steps // 2)
    launch(1)
    scatter(2, 1, steps // 2, steps)
    store_grid(2)

    @pl.loop(0, groups)
    def _(k):
        send_grid(2 * SPLIT, k)

    relay(0)
    relay(1)

    @pl.loop(0, groups)
    def _(k):
        send_grid(2 * SPLIT + 1, k)

    launch(2)
    launch(3)
    for i in range(2, 6):
        relay(i)
    launch(4)
    relay(6)
    relay(7)
    launch(5)
    encode_pieces(0, 2)
    encode_pieces(2, 4)
    relay(8)
    relay(9)
    encode_pieces(4, 6)
    encode_pieces(6, 8)
    relay(10)
    relay(11)
    encode_pieces(8, 10)
    encode_pieces(10, 12)

    pltpu.make_async_copy(s1.at[pl.ds(0, nb - 1)], r1.at[pl.ds(0, nb - 1)], send1).wait()
    for h in range(PARTS * SPLIT):
        sent = grid.at[h, pl.ds(0, nb - 1)]
        pltpu.make_async_copy(sent, sent, send2.at[h]).wait()
    sent = spec.at[pl.ds(0, 3)]
    pltpu.make_async_copy(sent, sent, send3).wait()


def on_device(nb, ny, obs_vals, obs_colat, obs_lon, band_list, counts, w_in, b_in, w_out, b_out):
    obs = obs_vals.shape[2]
    modes = nb * LAT
    outs = w_out.shape[1]
    part_cols = CH * LON // PARTS
    send_cols = part_cols // SPLIT
    groups = nb // GROUP
    dma = pltpu.SemaphoreType.DMA
    vmem = pl.BlockSpec(memory_space=pltpu.VMEM)
    args = (
        obs_vals[0],
        obs_colat.reshape(obs // CAP, CAP),
        obs_lon.reshape(obs // CAP, CAP),
        band_list[0],
        counts,
        jnp.asarray(cheb_inverse().T),
        jnp.asarray(dct_columns(modes)).astype(BF16),
        w_in,
        b_in[None, :],
        w_out.T,
        b_out[None, :],
    )
    return pl.pallas_call(
        functools.partial(kernel, nb, ny),
        out_shape=jax.ShapeDtypeStruct((outs, LON, modes), BF16),
        in_specs=[pl.BlockSpec(memory_space=pltpu.HBM)] * INPUTS,
        out_specs=vmem,
        scratch_shapes=[
            *(pltpu.VMEM(arg.shape, arg.dtype) for arg in args),
            pltpu.VMEM((nb, 1), F32),
            pltpu.VMEM((outs, 1), F32),
            pltpu.VMEM((obs // LANES * AUX, LANES), BF16),
            pltpu.VMEM((nb, AUX, CAP), BF16),
            pltpu.VMEM((nb, AUX, CAP), BF16),
            pltpu.VMEM((nb, 4 * LAT + 4 * CH, CAP), F32),
            pltpu.VMEM((nb * LAT, part_cols), F32),
            pltpu.VMEM((PARTS * SPLIT, nb, LAT, send_cols), BF16),
            pltpu.VMEM((PARTS * SPLIT, nb, LAT, send_cols), BF16),
            pltpu.VMEM((ny, LON * CH, modes), BF16),
            pltpu.VMEM((2 * w_in.shape[1], 2 * w_in.shape[0] + 16), BF16),
            pltpu.VMEM((outs, w_out.shape[0]), BF16),
            pltpu.VMEM((STRIPS, 2 * w_in.shape[1], modes // STRIPS), F32),
            pltpu.VMEM((outs, LON, modes), F32),
            dma((INPUTS,)), dma, dma((groups,)), dma((PARTS * SPLIT,)), dma((PARTS * SPLIT,)),
            dma, dma((PIECES,)), dma((PIECES,)), dma((PIECES,)),
        ],
        compiler_params=pltpu.CompilerParams(
            collective_id=0, has_side_effects=True, vmem_limit_bytes=40 * 1024 * 1024
        ),
    )(*(pltpu.with_memory_space_constraint(arg, pltpu.HBM) for arg in args))


def solution(mesh):
    nb, ny = mesh.shape["band"], mesh.shape["lev"]
    in_specs = (
        P("lev", None, "band"),
        P("band"),
        P("band"),
        P("band", None, None),
        P("band", None),
        P(),
        P(),
        P(None, "lev"),
        P("lev"),
    )
    return jax.shard_map(
        functools.partial(on_device, nb, ny),
        mesh=mesh, in_specs=in_specs, out_specs=P("lev", "band", None), check_vma=False,
    )
```
